128 devices in a mesh: slide: 4 (over x), gy: 8 (over z_lo, y), gx: 4 (over z_hi, core).
Axes of the slice: x: 4, y: 4, z: 4 (z_hi: 2, z_lo: 2; z = z_hi * 2 + z_lo), core: 2. Of those that a mesh axis runs over, the one named last changes fastest.
Arguments:
- tokens: bfloat16 [4, 128, 64, 1024], P('slide', 'gy', 'gx'), may hold values from -64 to 64, as said below
- weights: bfloat16 [1024, 4096], replicated, may hold values from -5 to 5
- norm_gain: float32 [1024], replicated, may hold values from 0.25 to 1.75
- tissue: int32 [4, 128, 64], P('slide', 'gy', 'gx'), may hold values from 0 to 1, as said below
- cotangent: bfloat16 [4, 128, 64, 1024], P('slide', 'gy', 'gx'), may hold values from -6 to 6
Outputs:
- block_output: bfloat16 [4, 128, 64, 1024], P('slide', 'gy', 'gx')
- input_grad: bfloat16 [4, 128, 64, 1024], P('slide', 'gy', 'gx')
- weight_grads: float32 [1024, 4096], P(('slide', 'gy', 'gx'))
The draws below stay inside these ranges and needn't reach their ends.
Inputs may be any that keep to these rules, and one draw needn't show every extreme that they name: `tokens`: token activations. 1 marks a tissue token, 0 background.
All inputs are finite; a program needn't handle non-finite values.
Results may differ from the reference program's by a relative error of at most 0.015.
The reference program's roundings to bfloat16 on the way count: a program that leaves them out, or rounds other values in their place, can miss the bound.
Values may be sent and summed in bfloat16 or wider, within the bound.
A program may use at most 128 MiB of HBM per device.

```python
import math
import jax
import jax.numpy as jnp
from jax import lax

D = 1024
HEADS = 16
RADIUS = 6
SLIDES = 4
NY = 128
NX = 64
ALL_TOKENS = 32768


def draw_tokens(key, part):
    first_key = jax.random.fold_in(key, 0)
    drawn = jnp.clip(jax.random.normal(first_key, (SLIDES, NY, NX, D), jnp.float32), -6.0, 6.0)
    return drawn.astype(jnp.bfloat16)


def draw_weights(key, part):
    drawn = jnp.clip(jax.random.normal(key, (D, 4 * D), jnp.float32), -6.0, 6.0)
    column = jnp.arange(4 * D)
    quarter = column // D
    factor = jnp.where(quarter < 2, 1.3, jnp.where(quarter == 2, 1.0, 4.0))
    return (drawn * factor[None, :] / math.sqrt(D)).astype(jnp.bfloat16)


def draw_tissue(key, part):
    subkeys = jax.random.split(key, 5)
    row_index = jnp.arange(NY)[None, :, None]
    col_index = jnp.arange(NX)[None, None, :]
    centre_rows = jax.random.randint(subkeys[0], (3, SLIDES, 1, 1), 1, NY)
    centre_cols = jax.random.randint(subkeys[1], (3, SLIDES, 1, 1), 1, NX)
    radius_rows = jax.random.randint(subkeys[2], (3, SLIDES, 1, 1), NY // 8 + 1, NY // 3 + 2)
    radius_cols = jax.random.randint(subkeys[3], (3, SLIDES, 1, 1), NX // 8 + 1, NX // 3 + 2)
    covered = jnp.zeros((SLIDES, NY, NX), bool)
    for blob_index in range(3):
        down = row_index - centre_rows[blob_index]
        across = col_index - centre_cols[blob_index]
        inside = down * down * 64 // (radius_rows[blob_index] * radius_rows[blob_index]) + across * across * 64 // (radius_cols[blob_index] * radius_cols[blob_index]) <= 64
        covered = covered | inside
    holes = jax.random.randint(subkeys[4], (SLIDES, NY, NX), 0, 8) != 0
    result = covered & holes
    result = result | (row_index == centre_rows[0]) & (col_index == centre_cols[0])
    result = result & jnp.logical_not((row_index == 0) & (col_index == 0))
    return result.astype(jnp.int32)


def block_levels(stream_key, extent, shards, low, largest):
    def one(dim, shards_of):
        steps = jax.random.uniform(jax.random.fold_in(jax.random.fold_in(stream_key, 6), dim), (shards_of,), jnp.float32, low / len(shards), largest / len(shards))
        return jnp.repeat(jnp.exp(steps), extent[dim] // shards_of).reshape((-1,) + (1,) * (len(extent) - dim - 1))

    gain = one(*shards[0])
    for cut in shards[1:]:
        gain = gain * one(*cut)
    return gain


def normal_values(stream_key, shape, spread, reach, pieces=(), dtype=jnp.bfloat16):
    values = jax.random.normal(stream_key, shape, jnp.float32) * spread
    if len(pieces) > 0:
        values = block_levels(stream_key, shape, pieces, -0.22, 0.18) * values
    return jnp.clip(values, min=-reach, max=reach).astype(dtype)


def setup_inputs(seed: int = 0) -> dict:
    keys = jax.random.split(jax.random.key(seed), 6)
    return {
        "tokens": draw_tokens(jax.random.fold_in(keys[5], 71), 0),
        "weights": draw_weights(jax.random.fold_in(keys[5], 71), 0),
        "norm_gain": jnp.clip(1.0 + 0.15 * jax.random.normal(keys[2], (D,), jnp.float32), 0.25, 1.75),
        "tissue": draw_tissue(jax.random.fold_in(keys[5], 71), 0),
        "cotangent": normal_values(keys[4], (SLIDES, NY, NX, D), 1.0, 6.0, ((0, 4), (1, 8), (2, 4))),
    }


EPSILON = 1e-06

def contract(pattern, left_operand, second):
    return jnp.einsum(pattern, left_operand.astype(jnp.float32), second.astype(jnp.float32))

def into_blocks(array, blocks_down, blocks_across, head_dim):
    shaped = array.reshape(blocks_down, 8, blocks_across, 8, HEADS, head_dim)
    return shaped.transpose(0, 2, 1, 3, 4, 5).reshape(blocks_down * blocks_across, 64, HEADS, head_dim)

def from_blocks(array, blocks_down, blocks_across):
    model_width = array.shape[2] * array.shape[3]
    shaped = array.reshape(blocks_down, blocks_across, 8, 8, model_width)
    return shaped.transpose(0, 2, 1, 3, 4).reshape(blocks_down * 8, blocks_across * 8, model_width)

def stack_windows(array, blocks_count):
    return jnp.stack([array[offset:offset + blocks_count] for offset in range(3)], axis=1)

def tile_attention(queries, key_values, grad_attn, row_valid, col_valid):
    tile_rows, tile_cols, model_width = queries.shape
    head_dim = model_width // HEADS
    blocks_down = tile_rows // 8
    blocks_across = tile_cols // 8
    block_count = blocks_down * blocks_across
    window_edge = 8 + 2 * RADIUS
    window_size = window_edge * window_edge
    extra_rows = 16 - 2 * RADIUS
    channels = key_values.shape[2]
    padded = jnp.pad(key_values, ((0, extra_rows), (0, extra_rows), (0, 0)))
    block_grid = padded.reshape(blocks_down + 2, 8, blocks_across + 2, 8, channels)
    row_stack = stack_windows(block_grid, blocks_down)
    full_stack = jnp.stack([row_stack[:, :, :, offset:offset + blocks_across] for offset in range(3)], axis=4)
    windows = full_stack.reshape(blocks_down, 24, blocks_across, 24, channels)[:, :window_edge, :, :window_edge]
    windows = windows.transpose(0, 2, 1, 3, 4).reshape(block_count, window_size, channels)
    row_padded = jnp.pad(row_valid, (0, extra_rows)).reshape(blocks_down + 2, 8)
    row_window = stack_windows(row_padded, blocks_down).reshape(blocks_down, 24)[:, :window_edge]
    col_padded = jnp.pad(col_valid, (0, extra_rows)).reshape(blocks_across + 2, 8)
    col_window = stack_windows(col_padded, blocks_across).reshape(blocks_across, 24)[:, :window_edge]
    query_slot = jnp.arange(64)
    key_slot = jnp.arange(window_size)
    query_row = (query_slot // 8)[:, None]
    query_col = (query_slot % 8)[:, None]
    key_row = (key_slot // window_edge)[None, :]
    key_col = (key_slot % window_edge)[None, :]
    nearby = (key_row >= query_row) & (key_row <= query_row + 2 * RADIUS)
    nearby = nearby & (key_col >= query_col) & (key_col <= query_col + 2 * RADIUS)
    in_grid = (row_window[:, None, :, None] & col_window[None, :, None, :]).reshape(block_count, 1, 1, window_size)
    allowed = nearby[None, None] & in_grid
    query_blocks = into_blocks(queries, blocks_down, blocks_across, head_dim)
    grad_blocks = into_blocks(grad_attn, blocks_down, blocks_across, head_dim)
    key_blocks = windows[:, :, :model_width].reshape(block_count, window_size, HEADS, head_dim)
    value_blocks = windows[:, :, model_width:].reshape(block_count, window_size, HEADS, head_dim)
    scaling = 1.0 / math.sqrt(head_dim)
    scores = contract('nqhd,nkhd->nhqk', query_blocks, key_blocks) * scaling
    scores = jnp.where(allowed, scores, -1e+30)
    row_max = lax.optimization_barrier(jnp.max(scores, axis=-1, keepdims=True))
    exponent = jnp.exp(scores - row_max)
    attn_probs = exponent / lax.optimization_barrier(jnp.sum(exponent, axis=-1, keepdims=True))
    probs_bf = attn_probs.astype(jnp.bfloat16)
    attended = contract('nhqk,nkhd->nqhd', probs_bf, value_blocks).astype(jnp.bfloat16)
    grad_probs = contract('nqhd,nkhd->nhqk', grad_blocks, value_blocks)
    centred = grad_probs - lax.optimization_barrier(jnp.sum(attn_probs * grad_probs, axis=-1, keepdims=True))
    grad_scores = (attn_probs * centred * scaling).astype(jnp.bfloat16)
    grad_queries = contract('nhqk,nkhd->nqhd', grad_scores, key_blocks).astype(jnp.bfloat16)
    grad_keys = contract('nhqk,nqhd->nkhd', grad_scores, query_blocks)
    grad_values = contract('nhqk,nqhd->nkhd', probs_bf, grad_blocks)
    grad_windows = jnp.concatenate([grad_keys.reshape(block_count, window_size, model_width), grad_values.reshape(block_count, window_size, model_width)], axis=-1)
    grad_windows = grad_windows.reshape(blocks_down, blocks_across, window_edge, window_edge, channels)
    grad_windows = jnp.pad(grad_windows, ((0, 0), (0, 0), (0, 24 - window_edge), (0, 24 - window_edge), (0, 0)))
    grad_windows = grad_windows.reshape(blocks_down, blocks_across, 3, 8, 3, 8, channels)
    accumulated = jnp.zeros((blocks_down + 2, 8, blocks_across + 2, 8, channels), jnp.float32)
    for offset_down in range(3):
        for offset_across in range(3):
            window_part = grad_windows[:, :, offset_down, :, offset_across].transpose(0, 2, 1, 3, 4)
            accumulated = accumulated.at[offset_down:offset_down + blocks_down, :, offset_across:offset_across + blocks_across].add(window_part)
    accumulated = accumulated.reshape(8 * (blocks_down + 2), 8 * (blocks_across + 2), channels)
    accumulated = accumulated[:tile_rows + 2 * RADIUS, :tile_cols + 2 * RADIUS]
    return (from_blocks(attended, blocks_down, blocks_across), from_blocks(grad_queries, blocks_down, blocks_across), accumulated)

def one_slide(slide_tokens, weights, norm_gain, slide_tissue, slide_cot):
    weight_in = weights[:, :3 * D]
    weight_out = weights[:, 3 * D:]
    tokens_float = slide_tokens.astype(jnp.float32)
    row_mean = lax.optimization_barrier(jnp.mean(tokens_float, axis=-1, keepdims=True))
    centered = tokens_float - row_mean
    variance = lax.optimization_barrier(jnp.mean(centered * centered, axis=-1, keepdims=True))
    inverse = lax.rsqrt(variance + EPSILON)
    normalized = centered * inverse
    normed = (normalized * norm_gain).astype(jnp.bfloat16)
    normed_flat = normed.reshape(NY * NX, D)
    projected = jnp.dot(normed_flat, weight_in, preferred_element_type=jnp.float32).astype(jnp.bfloat16).reshape(NY, NX, 3 * D)
    queries = projected[:, :, :D]
    key_values = projected[:, :, D:]
    tissue_mask = slide_tissue.astype(jnp.float32)[:, :, None]
    upstream = slide_cot.astype(jnp.float32)
    branch_grad = (tissue_mask * upstream).astype(jnp.bfloat16)
    branch_flat = branch_grad.reshape(NY * NX, D)
    grad_attn = jnp.dot(branch_flat, weight_out.T, preferred_element_type=jnp.float32).astype(jnp.bfloat16).reshape(NY, NX, D)
    padded_kv = jnp.pad(key_values, ((RADIUS, RADIUS), (RADIUS, RADIUS), (0, 0)))
    row_coord = jnp.arange(NY + 2 * RADIUS)
    row_valid = (row_coord >= RADIUS) & (row_coord < NY + RADIUS)
    col_coord = jnp.arange(NX + 2 * RADIUS)
    col_valid = (col_coord >= RADIUS) & (col_coord < NX + RADIUS)

    def strip_step(strip_index, carry):
        attended_all, grad_query_all, grad_padded_all = carry
        top_row = (strip_index * 8).astype(jnp.int32)
        query_strip = lax.dynamic_slice_in_dim(queries, top_row, 8, 0)
        kv_strip = lax.dynamic_slice_in_dim(padded_kv, top_row, 8 + 2 * RADIUS, 0)
        grad_strip = lax.dynamic_slice_in_dim(grad_attn, top_row, 8, 0)
        valid_strip = lax.dynamic_slice_in_dim(row_valid, top_row, 8 + 2 * RADIUS, 0)
        attended, grad_queries, grad_padded = tile_attention(query_strip, kv_strip, grad_strip, valid_strip, col_valid)
        attended_all = lax.dynamic_update_slice_in_dim(attended_all, attended, top_row, 0)
        grad_query_all = lax.dynamic_update_slice_in_dim(grad_query_all, grad_queries, top_row, 0)
        previous = lax.dynamic_slice_in_dim(grad_padded_all, top_row, 8 + 2 * RADIUS, 0)
        grad_padded_all = lax.dynamic_update_slice_in_dim(grad_padded_all, previous + grad_padded, top_row, 0)
        return (attended_all, grad_query_all, grad_padded_all)
    start_carry = (jnp.zeros((NY, NX, D), jnp.bfloat16), jnp.zeros((NY, NX, D), jnp.bfloat16), jnp.zeros((NY + 2 * RADIUS, NX + 2 * RADIUS, 2 * D), jnp.float32))
    attended_all, grad_query_all, grad_padded_all = lax.fori_loop(0, NY // 8, strip_step, start_carry)
    grad_kv = grad_padded_all[RADIUS:RADIUS + NY, RADIUS:RADIUS + NX].astype(jnp.bfloat16)
    grad_projected = jnp.concatenate([grad_query_all, grad_kv], axis=-1).reshape(NY * NX, 3 * D)
    attended_flat = attended_all.reshape(NY * NX, D)
    projection = jnp.dot(attended_flat, weight_out, preferred_element_type=jnp.float32).reshape(NY, NX, D)
    block_output = (tokens_float + tissue_mask * projection).astype(jnp.bfloat16)
    grad_normed = jnp.dot(grad_projected, weight_in.T, preferred_element_type=jnp.float32).reshape(NY, NX, D)
    scaled = grad_normed * norm_gain
    first_mean = lax.optimization_barrier(jnp.mean(scaled, axis=-1, keepdims=True))
    second_mean = lax.optimization_barrier(jnp.mean(scaled * normalized, axis=-1, keepdims=True))
    input_grad = (upstream + inverse * (scaled - first_mean - normalized * second_mean)).astype(jnp.bfloat16)
    grad_in = jnp.dot(normed_flat.T, grad_projected, preferred_element_type=jnp.float32)
    grad_out = jnp.dot(attended_flat.T, branch_flat, preferred_element_type=jnp.float32)
    return (block_output, input_grad, jnp.concatenate([grad_in, grad_out], axis=1))

def reference(tokens, weights, norm_gain, tissue, cotangent):
    outputs_list = []
    grads_list = []
    grad_total = jnp.zeros((D, 4 * D), jnp.float32)
    for slide_index in range(SLIDES):
        block_output, input_grad, slide_grads = one_slide(tokens[slide_index], weights, norm_gain, tissue[slide_index], cotangent[slide_index])
        outputs_list.append(block_output)
        grads_list.append(input_grad)
        grad_total = grad_total + slide_grads
    inv_root = 1.0 / math.sqrt(ALL_TOKENS)
    return (jnp.stack(outputs_list), jnp.stack(grads_list), grad_total * inv_root)
```

```python
import functools
import math

import jax
import jax.numpy as jnp
from jax import lax
from jax.experimental import pallas as pl
from jax.experimental.pallas import tpu as pltpu
from jax.sharding import PartitionSpec as P

HEADS = 16
RADIUS = 6


EPSILON = 1e-06


def with_halo(block, sides, width):
    for axis, dim in sides:
        count = lax.axis_size(axis)
        forward = [(i, i + 1) for i in range(count - 1)]
        backward = [(target, source) for source, target in forward]
        low = lax.ppermute(
            lax.slice_in_dim(block, block.shape[dim] - width, None, axis=dim), axis, forward
        )
        high = lax.ppermute(lax.slice_in_dim(block, 0, width, axis=dim), axis, backward)
        block = jnp.concatenate([low, block, high], axis=dim)
    return block


def shifted(shard, axis, by):
    count = lax.axis_size(axis)
    pairs = [(i, i + by) for i in range(count) if 0 <= i + by < count]
    return lax.ppermute(shard, axis, pairs)


def contract(pattern, left_operand, second):
    return jnp.einsum(pattern, left_operand, second, preferred_element_type=jnp.float32)


def into_blocks(array, blocks_down, blocks_across, head_dim):
    shaped = array.reshape(blocks_down, 8, blocks_across, 8, HEADS, head_dim)
    return shaped.transpose(0, 2, 1, 3, 4, 5).reshape(
        blocks_down * blocks_across, 64, HEADS, head_dim
    )


def from_blocks(array, blocks_down, blocks_across):
    model_width = array.shape[2] * array.shape[3]
    shaped = array.reshape(blocks_down, blocks_across, 8, 8, model_width)
    return shaped.transpose(0, 2, 1, 3, 4).reshape(blocks_down * 8, blocks_across * 8, model_width)


def stack_windows(array, blocks_count):
    return jnp.stack([array[offset : offset + blocks_count] for offset in range(3)], axis=1)


def tile_attention(queries, key_values, grad_attn, row_valid, col_valid):
    tile_rows, tile_cols, model_width = queries.shape
    head_dim = model_width // HEADS
    blocks_down = tile_rows // 8
    blocks_across = tile_cols // 8
    block_count = blocks_down * blocks_across
    window_edge = 8 + 2 * RADIUS
    window_size = window_edge * window_edge
    extra_rows = 16 - 2 * RADIUS
    channels = key_values.shape[2]
    padded = jnp.pad(key_values, ((0, extra_rows), (0, extra_rows), (0, 0)))
    block_grid = padded.reshape(blocks_down + 2, 8, blocks_across + 2, 8, channels)
    row_stack = stack_windows(block_grid, blocks_down)
    full_stack = jnp.stack(
        [row_stack[:, :, :, offset : offset + blocks_across] for offset in range(3)], axis=4
    )
    windows = full_stack.reshape(blocks_down, 24, blocks_across, 24, channels)[
        :, :window_edge, :, :window_edge
    ]
    windows = windows.transpose(0, 2, 1, 3, 4).reshape(block_count, window_size, channels)
    row_padded = jnp.pad(row_valid, (0, extra_rows)).reshape(blocks_down + 2, 8)
    row_window = stack_windows(row_padded, blocks_down).reshape(blocks_down, 24)[:, :window_edge]
    col_padded = jnp.pad(col_valid, (0, extra_rows)).reshape(blocks_across + 2, 8)
    col_window = stack_windows(col_padded, blocks_across).reshape(blocks_across, 24)[
        :, :window_edge
    ]
    query_slot = jnp.arange(64)
    key_slot = jnp.arange(window_size)
    query_row = (query_slot // 8)[:, None]
    query_col = (query_slot % 8)[:, None]
    key_row = (key_slot // window_edge)[None, :]
    key_col = (key_slot % window_edge)[None, :]
    nearby = (key_row >= query_row) & (key_row <= query_row + 2 * RADIUS)
    nearby = nearby & (key_col >= query_col) & (key_col <= query_col + 2 * RADIUS)
    in_grid = (row_window[:, None, :, None] & col_window[None, :, None, :]).reshape(
        block_count, 1, 1, window_size
    )
    allowed = nearby[None, None] & in_grid
    query_blocks = into_blocks(queries, blocks_down, blocks_across, head_dim)
    grad_blocks = into_blocks(grad_attn, blocks_down, blocks_across, head_dim)
    key_blocks = windows[:, :, :model_width].reshape(block_count, window_size, HEADS, head_dim)
    value_blocks = windows[:, :, model_width:].reshape(block_count, window_size, HEADS, head_dim)
    scaling = 1.0 / math.sqrt(head_dim)
    scores = contract("nqhd,nkhd->nhqk", query_blocks, key_blocks) * scaling
    scores = jnp.where(allowed, scores, -1e30)
    row_max = jnp.max(scores, axis=-1, keepdims=True)
    exponent = jnp.exp(scores - row_max)
    attn_probs = exponent / jnp.sum(exponent, axis=-1, keepdims=True)
    probs_bf = attn_probs.astype(jnp.bfloat16)
    attended = contract("nhqk,nkhd->nqhd", probs_bf, value_blocks).astype(jnp.bfloat16)
    grad_probs = contract("nqhd,nkhd->nhqk", grad_blocks, value_blocks)
    centred = grad_probs - jnp.sum(attn_probs * grad_probs, axis=-1, keepdims=True)
    grad_scores = (attn_probs * centred * scaling).astype(jnp.bfloat16)
    grad_queries = contract("nhqk,nkhd->nqhd", grad_scores, key_blocks).astype(jnp.bfloat16)
    grad_keys = contract("nhqk,nqhd->nkhd", grad_scores, query_blocks)
    grad_values = contract("nhqk,nqhd->nkhd", probs_bf, grad_blocks)
    grad_windows = jnp.concatenate(
        [
            grad_keys.reshape(block_count, window_size, model_width),
            grad_values.reshape(block_count, window_size, model_width),
        ],
        axis=-1,
    )
    grad_windows = grad_windows.reshape(
        blocks_down, blocks_across, window_edge, window_edge, channels
    )
    grad_windows = jnp.pad(
        grad_windows, ((0, 0), (0, 0), (0, 24 - window_edge), (0, 24 - window_edge), (0, 0))
    )
    grad_windows = grad_windows.reshape(blocks_down, blocks_across, 3, 8, 3, 8, channels)
    accumulated = jnp.zeros((blocks_down + 2, 8, blocks_across + 2, 8, channels), jnp.float32)
    for offset_down in range(3):
        for offset_across in range(3):
            window_part = grad_windows[:, :, offset_down, :, offset_across].transpose(0, 2, 1, 3, 4)
            accumulated = accumulated.at[
                offset_down : offset_down + blocks_down,
                :,
                offset_across : offset_across + blocks_across,
            ].add(window_part)
    accumulated = accumulated.reshape(8 * (blocks_down + 2), 8 * (blocks_across + 2), channels)
    accumulated = accumulated[: tile_rows + 2 * RADIUS, : tile_cols + 2 * RADIUS]
    return (
        from_blocks(attended, blocks_down, blocks_across),
        from_blocks(grad_queries, blocks_down, blocks_across),
        accumulated,
    )


def run_strips(queries, padded_kv, grad_attn, row_valid, col_valid):
    tile_rows, tile_cols, model_width = queries.shape

    def strip_step(strip_index, carry):
        attended_all, grad_query_all, grad_padded_all = carry
        top_row = (strip_index * 8).astype(jnp.int32)
        query_strip = lax.dynamic_slice_in_dim(queries, top_row, 8, 0)
        kv_strip = lax.dynamic_slice_in_dim(padded_kv, top_row, 8 + 2 * RADIUS, 0)
        grad_strip = lax.dynamic_slice_in_dim(grad_attn, top_row, 8, 0)
        valid_strip = lax.dynamic_slice_in_dim(row_valid, top_row, 8 + 2 * RADIUS, 0)
        attended, grad_queries, grad_padded = tile_attention(
            query_strip, kv_strip, grad_strip, valid_strip, col_valid
        )
        attended_all = lax.dynamic_update_slice_in_dim(attended_all, attended, top_row, 0)
        grad_query_all = lax.dynamic_update_slice_in_dim(grad_query_all, grad_queries, top_row, 0)
        previous = lax.dynamic_slice_in_dim(grad_padded_all, top_row, 8 + 2 * RADIUS, 0)
        grad_padded_all = lax.dynamic_update_slice_in_dim(
            grad_padded_all, previous + grad_padded, top_row, 0
        )
        return (attended_all, grad_query_all, grad_padded_all)

    start_carry = (
        jnp.zeros((tile_rows, tile_cols, model_width), jnp.bfloat16),
        jnp.zeros((tile_rows, tile_cols, model_width), jnp.bfloat16),
        jnp.zeros((tile_rows + 2 * RADIUS, tile_cols + 2 * RADIUS, 2 * model_width), jnp.float32),
    )
    return lax.fori_loop(0, tile_rows // 8, strip_step, start_carry)


COLOR_COLS = ((0, 768), (768, 768), (1536, 512))
COLOR_AXES = ("xyz", "yzx", "zxy")


def coords():
    x = lax.axis_index("slide")
    gy = lax.axis_index("gy")
    gx = lax.axis_index("gx")
    zlo, y = gy // 4, gy % 4
    zhi, core = gx // 2, gx % 2
    return x, y, zhi * 2 + zlo, core


def device_at(x, y, z, core):
    return (x, (z % 2) * 4 + y, (z // 2) * 2 + core)


def neighbour(axis, by):
    x, y, z, core = coords()
    if axis == "x":
        return device_at((x + by + 4) % 4, y, z, core)
    if axis == "y":
        return device_at(x, (y + by + 4) % 4, z, core)
    return device_at(x, y, (z + by + 4) % 4, core)


def mate_id():
    x, y, z, core = coords()
    return device_at(x, y, z, 1 - core)


def axis_coord(axis):
    x, y, z, _ = coords()
    return {"x": x, "y": y, "z": z}[axis]


def pick(ref, left, axis, j):
    dims = [d for d in ("x", "l", "y", "h") if (d in left) or (d in "lh" and "z" in left)]
    index = []
    for d in dims:
        if d == axis:
            index.append(j)
        elif axis == "z" and d == "l":
            index.append(j % 2)
        elif axis == "z" and d == "h":
            index.append(j // 2)
        else:
            index.append(slice(None))
    return tuple(index)


def row_dims(left):
    out = []
    if "x" in left:
        out.append(4)
    if "z" in left:
        out.append(2)
    if "y" in left:
        out.append(4)
    if "z" in left:
        out.append(2)
    return tuple(out)


def remote(src, dst, ssem, rsem, dev):
    return pltpu.make_async_remote_copy(
        src_ref=src, dst_ref=dst, send_sem=ssem, recv_sem=rsem,
        device_id=dev, device_id_type=pl.DeviceIdType.MESH,
    )


def scatter_kernel(inv_root, normed, attended, gproj, branch, out, *scratch):
    (at_own, at_mate, b_own, b_mate, last_send, last_recv, mate_ss, mate_rs, ring_ss, ring_rs) = scratch[:10]
    bufs = scratch[10:]
    sbuf = [[bufs[c * 3 + p] for p in range(3)] for c in range(3)]
    rbuf = [[bufs[9 + c * 3 + p] for p in range(3)] for c in range(3)]
    keep = [[bufs[18 + c * 3 + p] for p in range(3)] for c in range(3)]
    acc = [[bufs[27 + c * 4 + p] for p in range(4)] for c in range(3)]
    core = coords()[3]

    barrier = pltpu.get_barrier_semaphore()
    partners = [mate_id()] + [neighbour(a, s) for a in "xyz" for s in (1, -1)]
    for dev in partners:
        pl.semaphore_signal(barrier, inc=1, device_id=dev, device_id_type=pl.DeviceIdType.MESH)
    pl.semaphore_wait(barrier, len(partners))

    mate_copies = []
    for j in range(4):
        src = gproj if j < 3 else branch
        base = j * 1024 if j < 3 else 0
        cols = pl.ds(pl.multiple_of(base + (1 - core) * 512, 512), 512)
        mate_copies.append(remote(src.at[:, cols], b_mate.at[j], mate_ss.at[j], mate_rs.at[j], mate_id()))
        mate_copies[-1].start()
    for kind, src in enumerate((normed, attended)):
        at_own[kind] = src[...].T.reshape(at_own.shape[1:])
        mate_copies.append(
            remote(at_own.at[kind], at_mate.at[kind], mate_ss.at[4 + kind], mate_rs.at[4 + kind], mate_id())
        )
        mate_copies[-1].start()
    for j in range(4):
        src = gproj if j < 3 else branch
        base = j * 1024 if j < 3 else 0
        cols = pl.ds(pl.multiple_of(base + core * 512, 512), 512)
        b_own[:, j * 512 : (j + 1) * 512] = src[:, cols]
    for copy in mate_copies:
        copy.wait_recv()

    def first_block(c, j):
        start, count = COLOR_COLS[c]
        axis = COLOR_AXES[c][0]
        kind = 1 if c == 2 else 0
        index = pick(None, "xyz", axis, j)
        left_own = at_own[(kind,) + index].reshape(256, 256)
        left_mate = at_mate[(kind,) + index].reshape(256, 256)
        total = jnp.dot(left_own, b_own[:, start : start + count], preferred_element_type=jnp.float32)
        parts = []
        for chunk in range(4):
            lo, hi = max(start, chunk * 512), min(start + count, (chunk + 1) * 512)
            if lo < hi:
                parts.append(
                    jnp.dot(
                        left_mate,
                        b_mate[chunk, :, lo - chunk * 512 : hi - chunk * 512],
                        preferred_element_type=jnp.float32,
                    )
                )
        return total + jnp.concatenate(parts, axis=1)

    for p in range(3):
        copies = [[None] * 6 for _ in range(3)]

        def send(c, s):
            axis = COLOR_AXES[c][p]
            by = 1 if s in (0, 2, 4) else -1
            copies[c][s] = remote(
                sbuf[c][p].at[s], rbuf[c][p].at[s],
                ring_ss.at[c, p, s], ring_rs.at[c, p, s], neighbour(axis, by),
            )
            copies[c][s].start()

        def block(c, by):
            axis = COLOR_AXES[c][p]
            j = (axis_coord(axis) + by + 4) % 4
            if p == 0:
                return first_block(c, j)
            ref = acc[c][p - 1]
            rows = 256 >> (2 * p)
            return ref[pick(None, COLOR_AXES[c][p:], axis, j)].reshape(rows, COLOR_COLS[c][1])

        for c in range(3):
            half = COLOR_COLS[c][1] // 2
            value = block(c, 2)
            sbuf[c][p][0] = value[:, :half].astype(jnp.bfloat16)
            send(c, 0)
            sbuf[c][p][1] = value[:, half:].astype(jnp.bfloat16)
            send(c, 1)
        for c in range(3):
            half = COLOR_COLS[c][1] // 2
            value = block(c, 1)
            sbuf[c][p][2] = value[:, half:].astype(jnp.bfloat16)
            send(c, 2)
            keep[c][p][0] = value[:, :half]
            value = block(c, -1)
            sbuf[c][p][3] = value[:, :half].astype(jnp.bfloat16)
            send(c, 3)
            keep[c][p][1] = value[:, half:]
        own = []
        for c in range(3):
            rows = 256 >> (2 * p)
            shape = acc[c][p].shape
            acc[c][p][...] = block(c, 0).reshape(shape)
        for c in range(3):
            for s in (0, 1):
                copies[c][s].wait_recv()
                sbuf[c][p][4 + s] = (keep[c][p][s] + rbuf[c][p][s].astype(jnp.float32)).astype(jnp.bfloat16)
                send(c, 4 + s)
        for c in range(3):
            half = COLOR_COLS[c][1] // 2
            for s in (2, 3, 4, 5):
                copies[c][s].wait_recv()
            shape = acc[c][p].shape
            lead = shape[:-1]
            first = rbuf[c][p][3].astype(jnp.float32) + rbuf[c][p][4].astype(jnp.float32)
            second = rbuf[c][p][2].astype(jnp.float32) + rbuf[c][p][5].astype(jnp.float32)
            acc[c][p][..., :half] += first.reshape(lead + (half,))
            acc[c][p][..., half:] += second.reshape(lead + (half,))
        for c in range(3):
            for s in range(6):
                copies[c][s].wait_send()

    for c in range(3):
        start, count = COLOR_COLS[c]
        value = acc[c][2][...] * inv_root
        mine = jnp.where(core == 0, value[:8], value[8:])
        theirs = jnp.where(core == 0, value[8:], value[:8])
        last_send[:, start : start + count] = theirs
        for chunk in range(4):
            lo, hi = max(start, chunk * 512), min(start + count, (chunk + 1) * 512)
            if lo < hi:
                offset = pl.multiple_of(chunk * 1024 + lo - chunk * 512 + core * 512, 256)
                out[:, pl.ds(offset, hi - lo)] = mine[:, lo - start : hi - start]
    final = remote(last_send, last_recv, mate_ss.at[6], mate_rs.at[6], mate_id())
    final.start()
    final.wait_recv()
    for chunk in range(4):
        offset = pl.multiple_of(chunk * 1024 + (1 - core) * 512, 512)
        out[:, pl.ds(offset, 512)] = last_recv[:, chunk * 512 : (chunk + 1) * 512]
    final.wait_send()
    for copy in mate_copies:
        copy.wait_send()


def scatter_weight_grads(normed, attended, gproj, branch, inv_root):
    bf16, f32 = jnp.bfloat16, jnp.float32
    scratch = [
        pltpu.VMEM((2, 4, 2, 4, 2, 16, 256), bf16),
        pltpu.VMEM((2, 4, 2, 4, 2, 16, 256), bf16),
        pltpu.VMEM((256, 2048), bf16),
        pltpu.VMEM((4, 256, 512), bf16),
        pltpu.VMEM((8, 2048), f32),
        pltpu.VMEM((8, 2048), f32),
        pltpu.SemaphoreType.DMA((7,)),
        pltpu.SemaphoreType.DMA((7,)),
        pltpu.SemaphoreType.DMA((3, 3, 6)),
        pltpu.SemaphoreType.DMA((3, 3, 6)),
    ]
    for _ in range(2):
        for c in range(3):
            for p in range(3):
                scratch.append(pltpu.VMEM((6, 256 >> (2 * p), COLOR_COLS[c][1] // 2), bf16))
    for c in range(3):
        for p in range(3):
            scratch.append(pltpu.VMEM((2, 256 >> (2 * p), COLOR_COLS[c][1] // 2), f32))
    for c in range(3):
        for p in range(4):
            left = COLOR_AXES[c][p + 1 :]
            scratch.append(pltpu.VMEM(row_dims(left) + (16, COLOR_COLS[c][1]), f32))
    return pl.pallas_call(
        functools.partial(scatter_kernel, inv_root),
        out_shape=jax.ShapeDtypeStruct((8, 4096), f32),
        in_specs=[pl.BlockSpec(memory_space=pltpu.VMEM)] * 4,
        out_specs=pl.BlockSpec(memory_space=pltpu.VMEM),
        scratch_shapes=scratch,
        compiler_params=pltpu.CompilerParams(
            collective_id=0, has_side_effects=True, vmem_limit_bytes=60 << 20
        ),
    )(normed, attended, gproj, branch)


def local(tokens, weights, norm_gain, tissue, cotangent):
    tile_tokens = tokens[0]
    tile_rows, tile_cols, model_width = tile_tokens.shape
    token_count = tile_rows * tile_cols
    group_count = lax.axis_size("slide") * lax.axis_size("gy") * lax.axis_size("gx")
    weight_in = weights[:, : 3 * model_width]
    weight_out = weights[:, 3 * model_width :]
    tokens_float = tile_tokens.astype(jnp.float32)
    row_mean = jnp.mean(tokens_float, axis=-1, keepdims=True)
    centered = tokens_float - row_mean
    variance = jnp.mean(centered * centered, axis=-1, keepdims=True)
    inverse = lax.rsqrt(variance + EPSILON)
    normalized = centered * inverse
    normed = (normalized * norm_gain).astype(jnp.bfloat16)
    normed_flat = normed.reshape(token_count, model_width)
    projected = jnp.dot(normed_flat, weight_in, preferred_element_type=jnp.float32).astype(
        jnp.bfloat16
    )
    projected = projected.reshape(tile_rows, tile_cols, 3 * model_width)
    queries = projected[:, :, :model_width]
    key_values = projected[:, :, model_width:]
    tissue_tile = tissue[0]
    tissue_mask = tissue_tile.astype(jnp.float32)[:, :, None]
    upstream = cotangent[0].astype(jnp.float32)
    branch_grad = (tissue_mask * upstream).astype(jnp.bfloat16)
    branch_flat = branch_grad.reshape(token_count, model_width)
    grad_attn = jnp.dot(branch_flat, weight_out.T, preferred_element_type=jnp.float32).astype(
        jnp.bfloat16
    )
    grad_attn = grad_attn.reshape(tile_rows, tile_cols, model_width)
    padded_kv = with_halo(key_values, (("gy", 0), ("gx", 1)), RADIUS)
    row_coord = jnp.arange(tile_rows + 2 * RADIUS) + lax.axis_index("gy") * tile_rows - RADIUS
    row_valid = (row_coord >= 0) & (row_coord < tile_rows * lax.axis_size("gy"))
    col_coord = jnp.arange(tile_cols + 2 * RADIUS) + lax.axis_index("gx") * tile_cols - RADIUS
    col_valid = (col_coord >= 0) & (col_coord < tile_cols * lax.axis_size("gx"))
    operands = (queries, padded_kv, grad_attn, row_valid, col_valid)
    attended, grad_queries, grad_padded = run_strips(*operands)
    attended_flat = attended.reshape(token_count, model_width)
    inv_root = 1.0 / math.sqrt(group_count * token_count)
    projection = jnp.dot(attended_flat, weight_out, preferred_element_type=jnp.float32)
    block_output = (
        tokens_float + tissue_mask * projection.reshape(tile_rows, tile_cols, model_width)
    ).astype(jnp.bfloat16)
    column_fold = grad_padded[:, RADIUS : RADIUS + tile_cols]
    for shift_by, rim_part in (
        (-1, grad_padded[:, :RADIUS]),
        (1, grad_padded[:, RADIUS + tile_cols :]),
    ):
        arrived = shifted(rim_part.astype(jnp.bfloat16), "gx", shift_by).astype(rim_part.dtype)
        if shift_by < 0:
            column_fold = column_fold.at[:, tile_cols - RADIUS :].add(arrived)
        else:
            column_fold = column_fold.at[:, :RADIUS].add(arrived)
    row_fold = column_fold[RADIUS : RADIUS + tile_rows]
    for shift_by, rim_part in ((-1, column_fold[:RADIUS]), (1, column_fold[RADIUS + tile_rows :])):
        arrived = shifted(rim_part.astype(jnp.bfloat16), "gy", shift_by).astype(rim_part.dtype)
        if shift_by < 0:
            row_fold = row_fold.at[tile_rows - RADIUS :].add(arrived)
        else:
            row_fold = row_fold.at[:RADIUS].add(arrived)
    grad_kv = row_fold.astype(jnp.bfloat16)
    grad_projected = jnp.concatenate([grad_queries, grad_kv], axis=-1).reshape(
        token_count, 3 * model_width
    )
    grad_normed = jnp.dot(grad_projected, weight_in.T, preferred_element_type=jnp.float32)
    grad_normed = grad_normed.reshape(tile_rows, tile_cols, model_width)
    scaled = grad_normed * norm_gain
    first_mean = jnp.mean(scaled, axis=-1, keepdims=True)
    second_mean = jnp.mean(scaled * normalized, axis=-1, keepdims=True)
    input_grad = (upstream + inverse * (scaled - first_mean - normalized * second_mean)).astype(
        jnp.bfloat16
    )
    weight_grads = scatter_weight_grads(
        normed_flat, attended_flat, grad_projected, branch_flat, inv_root
    )
    return (block_output[None], input_grad[None], weight_grads)


def solution(mesh):
    in_specs = (
        P("slide", "gy", "gx", None),
        P(),
        P(),
        P("slide", "gy", "gx"),
        P("slide", "gy", "gx", None),
    )
    out_specs = (
        P("slide", "gy", "gx", None),
        P("slide", "gy", "gx", None),
        P(("slide", "gy", "gx"), None),
    )
    return jax.shard_map(local, mesh=mesh, in_specs=in_specs, out_specs=out_specs, check_vma=False)
```

```python
import functools
import math

import jax
import jax.numpy as jnp
from jax import lax
from jax.experimental import pallas as pl
from jax.experimental.pallas import tpu as pltpu
from jax.sharding import PartitionSpec as P

EPSILON = 1e-06


COLOR_COLS = ((0, 768), (768, 768), (1536, 512))
COLOR_AXES = ("xyz", "yzx", "zxy")


def coords():
    x = lax.axis_index("slide")
    gy = lax.axis_index("gy")
    gx = lax.axis_index("gx")
    zlo, y = gy // 4, gy % 4
    zhi, core = gx // 2, gx % 2
    return x, y, zhi * 2 + zlo, core


def device_at(x, y, z, core):
    return (x, (z % 2) * 4 + y, (z // 2) * 2 + core)


def neighbour(axis, by):
    x, y, z, core = coords()
    if axis == "x":
        return device_at((x + by + 4) % 4, y, z, core)
    if axis == "y":
        return device_at(x, (y + by + 4) % 4, z, core)
    return device_at(x, y, (z + by + 4) % 4, core)


def mate_id():
    x, y, z, core = coords()
    return device_at(x, y, z, 1 - core)


def axis_coord(axis):
    x, y, z, _ = coords()
    return {"x": x, "y": y, "z": z}[axis]


def pick(ref, left, axis, j):
    dims = [d for d in ("x", "l", "y", "h") if (d in left) or (d in "lh" and "z" in left)]
    index = []
    for d in dims:
        if d == axis:
            index.append(j)
        elif axis == "z" and d == "l":
            index.append(j % 2)
        elif axis == "z" and d == "h":
            index.append(j // 2)
        else:
            index.append(slice(None))
    return tuple(index)


def row_dims(left):
    out = []
    if "x" in left:
        out.append(4)
    if "z" in left:
        out.append(2)
    if "y" in left:
        out.append(4)
    if "z" in left:
        out.append(2)
    return tuple(out)


def remote(src, dst, ssem, rsem, dev):
    return pltpu.make_async_remote_copy(
        src_ref=src, dst_ref=dst, send_sem=ssem, recv_sem=rsem,
        device_id=dev, device_id_type=pl.DeviceIdType.MESH,
    )


def scatter_kernel(inv_root, normed, attended, gproj, branch, out, *scratch):
    (at_own, at_mate, b_own, b_mate, last_send, last_recv, mate_ss, mate_rs, ring_ss, ring_rs) = scratch[:10]
    bufs = scratch[10:]
    sbuf = [[bufs[c * 3 + p] for p in range(3)] for c in range(3)]
    rbuf = [[bufs[9 + c * 3 + p] for p in range(3)] for c in range(3)]
    keep = [[bufs[18 + c * 3 + p] for p in range(3)] for c in range(3)]
    acc = [[bufs[27 + c * 4 + p] for p in range(4)] for c in range(3)]
    core = coords()[3]

    barrier = pltpu.get_barrier_semaphore()
    partners = [mate_id()] + [neighbour(a, s) for a in "xyz" for s in (1, -1)]
    for dev in partners:
        pl.semaphore_signal(barrier, inc=1, device_id=dev, device_id_type=pl.DeviceIdType.MESH)
    pl.semaphore_wait(barrier, len(partners))

    mate_copies = []
    for j in range(4):
        src = gproj if j < 3 else branch
        base = j * 1024 if j < 3 else 0
        cols = pl.ds(pl.multiple_of(base + (1 - core) * 512, 512), 512)
        mate_copies.append(remote(src.at[:, cols], b_mate.at[j], mate_ss.at[j], mate_rs.at[j], mate_id()))
        mate_copies[-1].start()
    for kind, src in enumerate((normed, attended)):
        at_own[kind] = src[...].T.reshape(at_own.shape[1:])
        mate_copies.append(
            remote(at_own.at[kind], at_mate.at[kind], mate_ss.at[4 + kind], mate_rs.at[4 + kind], mate_id())
        )
        mate_copies[-1].start()
    for j in range(4):
        src = gproj if j < 3 else branch
        base = j * 1024 if j < 3 else 0
        cols = pl.ds(pl.multiple_of(base + core * 512, 512), 512)
        b_own[:, j * 512 : (j + 1) * 512] = src[:, cols]
    for copy in mate_copies:
        copy.wait_recv()

    def first_block(c, j):
        start, count = COLOR_COLS[c]
        axis = COLOR_AXES[c][0]
        kind = 1 if c == 2 else 0
        index = pick(None, "xyz", axis, j)
        left_own = at_own[(kind,) + index].reshape(256, 256)
        left_mate = at_mate[(kind,) + index].reshape(256, 256)
        total = jnp.dot(left_own, b_own[:, start : start + count], preferred_element_type=jnp.float32)
        parts = []
        for chunk in range(4):
            lo, hi = max(start, chunk * 512), min(start + count, (chunk + 1) * 512)
            if lo < hi:
                parts.append(
                    jnp.dot(
                        left_mate,
                        b_mate[chunk, :, lo - chunk * 512 : hi - chunk * 512],
                        preferred_element_type=jnp.float32,
                    )
                )
        return total + jnp.concatenate(parts, axis=1)

    for p in range(3):
        copies = [[None] * 6 for _ in range(3)]

        def send(c, s):
            axis = COLOR_AXES[c][p]
            by = 1 if s in (0, 2, 4) else -1
            copies[c][s] = remote(
                sbuf[c][p].at[s], rbuf[c][p].at[s],
                ring_ss.at[c, p, s], ring_rs.at[c, p, s], neighbour(axis, by),
            )
            copies[c][s].start()

        def block(c, by):
            axis = COLOR_AXES[c][p]
            j = (axis_coord(axis) + by + 4) % 4
            if p == 0:
                return first_block(c, j)
            ref = acc[c][p - 1]
            rows = 256 >> (2 * p)
            return ref[pick(None, COLOR_AXES[c][p:], axis, j)].reshape(rows, COLOR_COLS[c][1])

        for c in range(3):
            half = COLOR_COLS[c][1] // 2
            value = block(c, 2)
            sbuf[c][p][0] = value[:, :half].astype(jnp.bfloat16)
            send(c, 0)
            sbuf[c][p][1] = value[:, half:].astype(jnp.bfloat16)
            send(c, 1)
        for c in range(3):
            half = COLOR_COLS[c][1] // 2
            value = block(c, 1)
            sbuf[c][p][2] = value[:, half:].astype(jnp.bfloat16)
            send(c, 2)
            keep[c][p][0] = value[:, :half]
            value = block(c, -1)
            sbuf[c][p][3] = value[:, :half].astype(jnp.bfloat16)
            send(c, 3)
            keep[c][p][1] = value[:, half:]
        own = []
        for c in range(3):
            rows = 256 >> (2 * p)
            shape = acc[c][p].shape
            acc[c][p][...] = block(c, 0).reshape(shape)
        for c in range(3):
            for s in (0, 1):
                copies[c][s].wait_recv()
                sbuf[c][p][4 + s] = (keep[c][p][s] + rbuf[c][p][s].astype(jnp.float32)).astype(jnp.bfloat16)
                send(c, 4 + s)
        for c in range(3):
            half = COLOR_COLS[c][1] // 2
            for s in (2, 3, 4, 5):
                copies[c][s].wait_recv()
            shape = acc[c][p].shape
            lead = shape[:-1]
            first = rbuf[c][p][3].astype(jnp.float32) + rbuf[c][p][4].astype(jnp.float32)
            second = rbuf[c][p][2].astype(jnp.float32) + rbuf[c][p][5].astype(jnp.float32)
            acc[c][p][..., :half] += first.reshape(lead + (half,))
            acc[c][p][..., half:] += second.reshape(lead + (half,))
        for c in range(3):
            for s in range(6):
                copies[c][s].wait_send()

    for c in range(3):
        start, count = COLOR_COLS[c]
        value = acc[c][2][...] * inv_root
        mine = jnp.where(core == 0, value[:8], value[8:])
        theirs = jnp.where(core == 0, value[8:], value[:8])
        last_send[:, start : start + count] = theirs
        for chunk in range(4):
            lo, hi = max(start, chunk * 512), min(start + count, (chunk + 1) * 512)
            if lo < hi:
                offset = pl.multiple_of(chunk * 1024 + lo - chunk * 512 + core * 512, 256)
                out[:, pl.ds(offset, hi - lo)] = mine[:, lo - start : hi - start]
    final = remote(last_send, last_recv, mate_ss.at[6], mate_rs.at[6], mate_id())
    final.start()
    final.wait_recv()
    for chunk in range(4):
        offset = pl.multiple_of(chunk * 1024 + (1 - core) * 512, 512)
        out[:, pl.ds(offset, 512)] = last_recv[:, chunk * 512 : (chunk + 1) * 512]
    final.wait_send()
    for copy in mate_copies:
        copy.wait_send()


def scatter_weight_grads(normed, attended, gproj, branch, inv_root):
    bf16, f32 = jnp.bfloat16, jnp.float32
    scratch = [
        pltpu.VMEM((2, 4, 2, 4, 2, 16, 256), bf16),
        pltpu.VMEM((2, 4, 2, 4, 2, 16, 256), bf16),
        pltpu.VMEM((256, 2048), bf16),
        pltpu.VMEM((4, 256, 512), bf16),
        pltpu.VMEM((8, 2048), f32),
        pltpu.VMEM((8, 2048), f32),
        pltpu.SemaphoreType.DMA((7,)),
        pltpu.SemaphoreType.DMA((7,)),
        pltpu.SemaphoreType.DMA((3, 3, 6)),
        pltpu.SemaphoreType.DMA((3, 3, 6)),
    ]
    for _ in range(2):
        for c in range(3):
            for p in range(3):
                scratch.append(pltpu.VMEM((6, 256 >> (2 * p), COLOR_COLS[c][1] // 2), bf16))
    for c in range(3):
        for p in range(3):
            scratch.append(pltpu.VMEM((2, 256 >> (2 * p), COLOR_COLS[c][1] // 2), f32))
    for c in range(3):
        for p in range(4):
            left = COLOR_AXES[c][p + 1 :]
            scratch.append(pltpu.VMEM(row_dims(left) + (16, COLOR_COLS[c][1]), f32))
    return pl.pallas_call(
        functools.partial(scatter_kernel, inv_root),
        out_shape=jax.ShapeDtypeStruct((8, 4096), f32),
        in_specs=[pl.BlockSpec(memory_space=pltpu.VMEM)] * 4,
        out_specs=pl.BlockSpec(memory_space=pltpu.VMEM),
        scratch_shapes=scratch,
        compiler_params=pltpu.CompilerParams(
            collective_id=0, has_side_effects=True, vmem_limit_bytes=60 << 20
        ),
    )(normed, attended, gproj, branch)


def dot_nn(left, right):
    return jnp.dot(left, right, preferred_element_type=jnp.float32)


def dot_nt(left, right):
    return lax.dot_general(left, right, (((1,), (1,)), ((), ())), preferred_element_type=jnp.float32)


def dot_tn(left, right):
    return lax.dot_general(left, right, (((0,), (0,)), ((), ())), preferred_element_type=jnp.float32)


def head_diagonal(full):
    low = lax.broadcasted_iota(jnp.int32, (64, 128), 1) < 64
    first = jnp.where(low, full[0:64, 0:128], full[64:128, 0:128])
    second = jnp.where(low, full[128:192, 128:256], full[192:256, 128:256])
    return jnp.concatenate([first, second], axis=1)


def attention_kernel(
    projected, projected_rows, grad_attn, attended, gproj,
    pad, queries, upstream, bias, acc,
    side_send, side_recv, back_send, back_recv, rows_send, rows_recv,
    load_sem, rows_ss, rows_rs, side_ss, side_rs, back_ss, back_rs, up_ss, up_rs,
):
    f32, bf16 = jnp.float32, jnp.bfloat16
    slide = lax.axis_index("slide")
    gy = lax.axis_index("gy")
    gx = lax.axis_index("gx")
    beside = ((slide, gy, gx - 1), (slide, gy, gx + 1))
    along = ((slide, gy - 1, gx), (slide, gy + 1, gx))
    has_beside = (gx > 0, gx < 3)
    has_along = (gy > 0, gy < 7)

    loads = []
    for g in range(4):
        for kv in range(2):
            lo = 1024 * (kv + 1) + 256 * g
            loads.append(
                pltpu.make_async_copy(
                    projected.at[:, :, lo : lo + 256], pad.at[g, kv, 6:22, 0:16, :], load_sem.at[2 * g + kv]
                )
            )
            loads[-1].start()
    query_load = pltpu.make_async_copy(projected_rows.at[:, :, 0:1024], queries, load_sem.at[8])
    query_load.start()
    upstream_load = pltpu.make_async_copy(grad_attn, upstream, load_sem.at[9])
    upstream_load.start()

    barrier = pltpu.get_barrier_semaphore()
    greeted = (
        (slide, gy, (gx + 3) % 4), (slide, gy, (gx + 1) % 4),
        (slide, (gy + 7) % 8, gx), (slide, (gy + 1) % 8, gx),
    )
    for dev in greeted:
        pl.semaphore_signal(barrier, inc=1, device_id=dev, device_id_type=pl.DeviceIdType.MESH)
    pl.semaphore_wait(barrier, 4)

    def rows_copy(g, side):
        src = (6, 16)[side]
        dst = (22, 0)[side]
        return remote(
            pad.at[g, :, src : src + 6, 0:16, :], pad.at[g, :, dst : dst + 6, 0:16, :],
            rows_ss.at[g, side], rows_rs.at[g, side], along[side],
        )

    def side_copy(g, side):
        return remote(
            side_send.at[g, side], side_recv.at[g, side], side_ss.at[g, side], side_rs.at[g, side], beside[side]
        )

    def back_copy(g, side):
        return remote(
            back_send.at[g, side], back_recv.at[g, side], back_ss.at[g, side], back_rs.at[g, side], beside[side]
        )

    def up_copy(g, side):
        return remote(
            rows_send.at[g, side], rows_recv.at[g, side], up_ss.at[g, side], up_rs.at[g, side], along[side]
        )

    for g in range(4):
        for kv in range(2):
            loads[2 * g + kv].wait()
        for side in range(2):
            @pl.when(has_along[side])
            def _(g=g, side=side):
                rows_copy(g, side).start()

    for b in range(4):
        shape = (512, 128)
        key = lax.broadcasted_iota(jnp.int32, shape, 0)
        lane = lax.broadcasted_iota(jnp.int32, shape, 1) & 63
        key_row, slot = key >> 5, key & 31
        key_col = jnp.where(slot < 24, slot, slot - 32)
        down = key_row - (lane >> 4)
        across = key_col - (lane & 15)
        grid_row = key_row + (gy * 16 + 4 * b - 6)
        grid_col = key_col + gx * 16
        allowed = (down >= 0) & (down <= 12) & (across >= -6) & (across <= 6)
        allowed = allowed & (grid_row >= 0) & (grid_row < 128) & (grid_col >= 0) & (grid_col < 64)
        half = jnp.where(allowed, 0.0, -1e30).astype(f32)
        bias[b] = jnp.concatenate([half, half], axis=1)

    query_load.wait()
    upstream_load.wait()

    for g in range(4):
        for side in range(2):
            zero_row = (22, 0)[side]

            @pl.when(has_along[side])
            def _(g=g, side=side):
                rows_copy(g, 1 - side).wait_recv()

            @pl.when(jnp.logical_not(has_along[side]))
            def _(g=g, zero_row=(0, 22)[side]):
                pad[g, :, zero_row : zero_row + 6, 0:16, :] = jnp.zeros((2, 6, 16, 256), bf16)

        inner = pad[g, :, :, 0:16, :].astype(f32)
        side_send[g, 0] = inner[:, :, 0:8, :].astype(bf16)
        side_send[g, 1] = inner[:, :, 8:16, :].astype(bf16)
        for side in range(2):
            @pl.when(has_beside[side])
            def _(g=g, side=side):
                side_copy(g, side).start()

    same_head = (lax.broadcasted_iota(jnp.int32, (256, 256), 0) >> 6) == (
        lax.broadcasted_iota(jnp.int32, (256, 256), 1) >> 6
    )
    head_mask = jnp.where(same_head, 1.0, 0.0).astype(bf16)

    def attend(g):
        columns = slice(256 * g, 256 * g + 256)
        acc[g] = jnp.zeros((2, 28, 32, 256), f32)

        def block(b, carry):
            keys = pad[g, 0, pl.ds(4 * b, 16)].reshape(512, 256)
            values = pad[g, 1, pl.ds(4 * b, 16)].reshape(512, 256)
            query = queries[b, :, columns] * jnp.asarray(0.125, bf16)
            grad = upstream[b, :, columns]
            query_heads = jnp.concatenate([query] * 4, axis=0) * head_mask
            grad_heads = jnp.concatenate([grad] * 4, axis=0) * head_mask
            scores = dot_nt(keys, query_heads) + bias[b]
            top = jnp.max(scores, axis=0, keepdims=True)
            exponent = jnp.exp(scores - top)
            total = jnp.sum(exponent, axis=0, keepdims=True)
            probs = exponent * (1.0 / total)
            probs_bf = probs.astype(bf16)
            grad_probs = dot_nt(values, grad_heads)
            centre = jnp.sum(probs * grad_probs, axis=0, keepdims=True)
            grad_scores = (probs * (grad_probs - centre)).astype(bf16)
            attended[b, :, columns] = head_diagonal(dot_tn(probs_bf, values)).astype(bf16)
            gproj[b, :, columns] = (head_diagonal(dot_tn(grad_scores, keys)) * 0.125).astype(bf16)
            rows = pl.ds(4 * b, 16)
            acc[g, 0, rows] += dot_nn(grad_scores, query_heads).reshape(16, 32, 256)
            acc[g, 1, rows] += dot_nn(probs_bf, grad_heads).reshape(16, 32, 256)
            return carry

        lax.fori_loop(0, 4, block, 0)

    def start_back(g):
        back_send[g, 0] = acc[g, :, :, 24:32, :].astype(bf16)
        back_send[g, 1] = acc[g, :, :, 16:24, :].astype(bf16)
        for side in range(2):
            @pl.when(has_beside[side])
            def _(side=side):
                back_copy(g, side).start()

    def start_up(g):
        for side in range(2):
            lo = (0, 8)[side]

            @pl.when(has_beside[side])
            def _(side=side, lo=lo):
                back_copy(g, 1 - side).wait_recv()
                acc[g, :, :, lo : lo + 8, :] += back_recv[g, 1 - side].astype(f32)

        rows_send[g, 0] = acc[g, :, 0:6, 0:16, :].astype(bf16)
        rows_send[g, 1] = acc[g, :, 22:28, 0:16, :].astype(bf16)
        for side in range(2):
            @pl.when(has_along[side])
            def _(side=side):
                up_copy(g, side).start()

    def finish(g):
        for side in range(2):
            lo = (6, 16)[side]

            @pl.when(has_along[side])
            def _(side=side, lo=lo):
                up_copy(g, 1 - side).wait_recv()
                acc[g, :, lo : lo + 6, 0:16, :] += rows_recv[g, 1 - side].astype(f32)

        for kv in range(2):
            lo = 1024 * (kv + 1) + 256 * g
            gproj[:, :, lo : lo + 256] = acc[g, kv, 6:22, 0:16, :].reshape(4, 64, 256).astype(bf16)

    for g in range(4):
        for side in range(2):
            @pl.when(has_beside[side])
            def _(g=g, side=side):
                side_copy(g, 1 - side).wait_recv()

            @pl.when(jnp.logical_not(has_beside[side]))
            def _(g=g, side=side):
                side_recv[g, 1 - side] = jnp.zeros((2, 28, 8, 256), bf16)

        outer = jnp.concatenate([side_recv[g, 0].astype(f32), side_recv[g, 1].astype(f32)], axis=2)
        pad[g, :, :, 16:32, :] = outer.astype(bf16)
        attend(g)
        start_back(g)
        if g >= 1:
            start_up(g - 1)
        if g >= 2:
            finish(g - 2)
    start_up(3)
    finish(2)
    finish(3)
    for g in range(4):
        for side in range(2):
            @pl.when(has_along[side])
            def _(g=g, side=side):
                rows_copy(g, side).wait_send()
                up_copy(g, side).wait_send()

            @pl.when(has_beside[side])
            def _(g=g, side=side):
                side_copy(g, side).wait_send()
                back_copy(g, side).wait_send()


def attention(projected, grad_attn):
    bf16, f32 = jnp.bfloat16, jnp.float32
    dma = pltpu.SemaphoreType.DMA
    any_space = pl.BlockSpec(memory_space=pl.ANY)
    vmem = pl.BlockSpec(memory_space=pltpu.VMEM)
    attended, gproj = pl.pallas_call(
        attention_kernel,
        out_shape=(
            jax.ShapeDtypeStruct((4, 64, 1024), bf16),
            jax.ShapeDtypeStruct((4, 64, 3072), bf16),
        ),
        in_specs=[any_space] * 3,
        out_specs=(vmem, vmem),
        scratch_shapes=[
            pltpu.VMEM((4, 2, 28, 32, 256), bf16),
            pltpu.VMEM((4, 64, 1024), bf16),
            pltpu.VMEM((4, 64, 1024), bf16),
            pltpu.VMEM((4, 512, 256), f32),
            pltpu.VMEM((4, 2, 28, 32, 256), f32),
            pltpu.VMEM((4, 2, 2, 28, 8, 256), bf16),
            pltpu.VMEM((4, 2, 2, 28, 8, 256), bf16),
            pltpu.VMEM((4, 2, 2, 28, 8, 256), bf16),
            pltpu.VMEM((4, 2, 2, 28, 8, 256), bf16),
            pltpu.VMEM((4, 2, 2, 6, 16, 256), bf16),
            pltpu.VMEM((4, 2, 2, 6, 16, 256), bf16),
            dma((10,)),
        ] + [dma((4, 2))] * 8,
        compiler_params=pltpu.CompilerParams(
            collective_id=1, has_side_effects=True, vmem_limit_bytes=62 << 20
        ),
    )(
        projected.reshape(16, 16, 3072),
        projected.reshape(4, 64, 3072),
        grad_attn.reshape(4, 64, 1024),
    )
    return attended.reshape(256, 1024), gproj.reshape(256, 3072)


def local(tokens, weights, norm_gain, tissue, cotangent):
    model_width = tokens.shape[-1]
    token_count = tokens.shape[1] * tokens.shape[2]
    group_count = lax.axis_size("slide") * lax.axis_size("gy") * lax.axis_size("gx")
    inv_root = 1.0 / math.sqrt(group_count * token_count)
    weight_in = weights[:, : 3 * model_width]
    weight_out = weights[:, 3 * model_width :]
    tokens_float = tokens.reshape(token_count, model_width).astype(jnp.float32)
    row_mean = jnp.mean(tokens_float, axis=-1, keepdims=True)
    centered = tokens_float - row_mean
    variance = jnp.mean(centered * centered, axis=-1, keepdims=True)
    inverse = lax.rsqrt(variance + EPSILON)
    normalized = centered * inverse
    normed = (normalized * norm_gain).astype(jnp.bfloat16)
    projected = jnp.dot(normed, weight_in, preferred_element_type=jnp.float32).astype(jnp.bfloat16)
    tissue_mask = tissue.reshape(token_count, 1).astype(jnp.float32)
    upstream = cotangent.reshape(token_count, model_width).astype(jnp.float32)
    branch_grad = (tissue_mask * upstream).astype(jnp.bfloat16)
    grad_attn = jnp.dot(branch_grad, weight_out.T, preferred_element_type=jnp.float32).astype(
        jnp.bfloat16
    )
    attended, grad_projected = attention(projected, grad_attn)
    projection = jnp.dot(attended, weight_out, preferred_element_type=jnp.float32)
    block_output = (tokens_float + tissue_mask * projection).astype(jnp.bfloat16)
    grad_normed = jnp.dot(grad_projected, weight_in.T, preferred_element_type=jnp.float32)
    scaled = grad_normed * norm_gain
    first_mean = jnp.mean(scaled, axis=-1, keepdims=True)
    second_mean = jnp.mean(scaled * normalized, axis=-1, keepdims=True)
    input_grad = (upstream + inverse * (scaled - first_mean - normalized * second_mean)).astype(
        jnp.bfloat16
    )
    weight_grads = scatter_weight_grads(normed, attended, grad_projected, branch_grad, inv_root)
    return (block_output.reshape(tokens.shape), input_grad.reshape(tokens.shape), weight_grads)


def solution(mesh):
    in_specs = (
        P("slide", "gy", "gx", None),
        P(),
        P(),
        P("slide", "gy", "gx"),
        P("slide", "gy", "gx", None),
    )
    out_specs = (
        P("slide", "gy", "gx", None),
        P("slide", "gy", "gx", None),
        P(("slide", "gy", "gx"), None),
    )
    return jax.shard_map(local, mesh=mesh, in_specs=in_specs, out_specs=out_specs, check_vma=False)
```

```python
import functools
import math

import jax
import jax.numpy as jnp
from jax import lax
from jax.experimental import pallas as pl
from jax.experimental.pallas import tpu as pltpu
from jax.sharding import PartitionSpec as P

EPSILON = 1e-06


LOADED_UP = 0
LOADED_DOWN = 3
CHUNK_AXES = ("xyz", "yzx", "zxy", "xzy")


def coords():
    x = lax.axis_index("slide")
    gy = lax.axis_index("gy")
    gx = lax.axis_index("gx")
    zlo, y = gy // 4, gy % 4
    zhi, core = gx // 2, gx % 2
    return x, y, zhi * 2 + zlo, core


def device_at(x, y, z, core):
    return (x, (z % 2) * 4 + y, (z // 2) * 2 + core)


def neighbour(axis, by):
    x, y, z, core = coords()
    if axis == "x":
        return device_at((x + by + 4) % 4, y, z, core)
    if axis == "y":
        return device_at(x, (y + by + 4) % 4, z, core)
    return device_at(x, y, (z + by + 4) % 4, core)


def mate_id():
    x, y, z, core = coords()
    return device_at(x, y, z, 1 - core)


def axis_coord(axis):
    x, y, z, _ = coords()
    return {"x": x, "y": y, "z": z}[axis]


def pick(ref, left, axis, j):
    dims = [d for d in ("x", "l", "y", "h") if (d in left) or (d in "lh" and "z" in left)]
    index = []
    for d in dims:
        if d == axis:
            index.append(j)
        elif axis == "z" and d == "l":
            index.append(j % 2)
        elif axis == "z" and d == "h":
            index.append(j // 2)
        else:
            index.append(slice(None))
    return tuple(index)


def row_dims(left):
    out = []
    if "x" in left:
        out.append(4)
    if "z" in left:
        out.append(2)
    if "y" in left:
        out.append(4)
    if "z" in left:
        out.append(2)
    return tuple(out)


def remote(src, dst, ssem, rsem, dev):
    return pltpu.make_async_remote_copy(
        src_ref=src, dst_ref=dst, send_sem=ssem, recv_sem=rsem,
        device_id=dev, device_id_type=pl.DeviceIdType.MESH,
    )


def dot_nn(left, right):
    return jnp.dot(left, right, preferred_element_type=jnp.float32)


def dot_nt(left, right):
    return lax.dot_general(left, right, (((1,), (1,)), ((), ())), preferred_element_type=jnp.float32)


def dot_tn(left, right):
    return lax.dot_general(left, right, (((0,), (0,)), ((), ())), preferred_element_type=jnp.float32)


def head_diagonal(full):
    low = lax.broadcasted_iota(jnp.int32, (64, 128), 1) < 64
    first = jnp.where(low, full[0:64, 0:128], full[64:128, 0:128])
    second = jnp.where(low, full[128:192, 128:256], full[192:256, 128:256])
    return jnp.concatenate([first, second], axis=1)


def pack_columns(slab):
    parts = slab.reshape(7, 4, 8, 128)
    place = lax.broadcasted_iota(jnp.int32, (7, 8, 128), 1)
    one = pltpu.roll(parts[:, 1], 6, 1)
    two = pltpu.roll(parts[:, 2], 4, 1)
    three = pltpu.roll(parts[:, 3], 2, 1)
    return (
        jnp.where(place < 6, parts[:, 0], one),
        jnp.where(place < 4, one, two),
        jnp.where(place < 2, two, three),
    )


def unpack_columns(first, second, third):
    place = lax.broadcasted_iota(jnp.int32, (7, 8, 128), 1)
    rows = (
        first,
        pltpu.roll(jnp.where(place < 4, second, first), 2, 1),
        pltpu.roll(jnp.where(place < 2, third, second), 4, 1),
        pltpu.roll(third, 6, 1),
    )
    return jnp.stack(rows, axis=1).reshape(28, 8, 128)


def sublayer_kernel(
    inv_root,
    projected, projected_rows, grad_attn, weights, normed, branch, tokens, cotangent, tissue, gain,
    block_output, input_grad, weight_grads,
    attended, gproj, weight_vmem, grad_normed,
    pad, queries, upstream, bias, acc,
    side_send, side_recv, back_send, back_recv, rows_send, rows_recv, side_relay, back_relay,
    at_own, at_mate, b_mate, last_send, last_recv,
    load_sem, rows_ss, rows_rs, up_ss, up_rs, side_ss, side_rs, back_ss, back_rs,
    far_ss, far_rs, far_relay_ss, far_relay_rs, farb_ss, farb_rs, farb_relay_ss, farb_relay_rs,
    swap_ss, swap_rs, grad_ss, grad_rs, ring_ss, ring_rs,
    *ring_bufs,
):
    f32, bf16 = jnp.float32, jnp.bfloat16
    slide = lax.axis_index("slide")
    gy = lax.axis_index("gy")
    gx = lax.axis_index("gx")
    _, y, z, core = coords()
    along = ((slide, gy - 1, gx), (slide, gy + 1, gx))
    has_along = (gy > 0, gy < 7)
    outer = (gx == 0) | (gx == 3)
    inner = jnp.logical_not(outer)
    mate = mate_id()
    signs = (1, jnp.where(y == LOADED_UP, -1, 1), jnp.where(y == LOADED_DOWN, 1, -1), -1)

    def opposite(by):
        other = (z + by + 4) % 4
        high = other // 2
        return (slide, (other % 2) * 4 + y, jnp.where(outer, high + 1, 3 * high))

    across = [opposite(sign) for sign in signs]

    loads = []
    for g in range(4):
        for kv in range(2):
            lo = 1024 * (kv + 1) + 256 * g
            loads.append(
                pltpu.make_async_copy(
                    projected.at[:, :, lo : lo + 256], pad.at[g, kv, 6:22, 0:16, :], load_sem.at[2 * g + kv]
                )
            )
            loads[-1].start()
    query_load = pltpu.make_async_copy(projected_rows.at[:, :, 0:1024], queries, load_sem.at[8])
    query_load.start()
    upstream_load = pltpu.make_async_copy(grad_attn, upstream, load_sem.at[9])
    upstream_load.start()
    weight_load = pltpu.make_async_copy(weights, weight_vmem, load_sem.at[10])
    weight_load.start()

    barrier = pltpu.get_barrier_semaphore()
    greeted = [mate, (slide, (gy + 7) % 8, gx), (slide, (gy + 1) % 8, gx), opposite(1), opposite(-1)]
    greeted += [neighbour(axis, by) for axis in "xyz" for by in (1, -1)]
    for dev in greeted:
        pl.semaphore_signal(barrier, inc=1, device_id=dev, device_id_type=pl.DeviceIdType.MESH)
    pl.semaphore_wait(barrier, len(greeted))

    def rows_copy(g, side):
        src = (6, 16)[side]
        dst = (22, 0)[side]
        return remote(
            pad.at[g, :, src : src + 6, 0:16, :], pad.at[g, :, dst : dst + 6, 0:16, :],
            rows_ss.at[g, side], rows_rs.at[g, side], along[side],
        )

    def mate_copy(g, sent, got, ss, rs):
        return remote(sent.at[g, 1 - core], got.at[g, 1 - core], ss.at[g], rs.at[g], mate)

    def far_copy(g, kv, sent, relay, ss, rs):
        return remote(sent.at[g, core, kv], relay.at[g, kv], ss.at[g, kv], rs.at[g, kv], across[kv])

    def relay_copy(g, kv, relay, got, ss, rs):
        source = (z - signs[kv] + 4) % 4
        return remote(
            relay.at[g, kv], got.at[g, 1 - source // 2, kv], ss.at[g, kv], rs.at[g, kv], across[kv]
        )

    def side_start(g):
        mate_copy(g, side_send, side_recv, side_ss, side_rs).start()

        @pl.when(inner)
        def _():
            for kv in range(4):
                far_copy(g, kv, side_send, side_relay, far_ss, far_rs).start()

    def side_forward(g):
        @pl.when(outer)
        def _():
            for kv in range(4):
                far_copy(g, kv, side_send, side_relay, far_ss, far_rs).wait_recv()
                relay_copy(g, kv, side_relay, side_recv, far_relay_ss, far_relay_rs).start()

    def side_wait(g):
        mate_copy(g, side_send, side_recv, side_ss, side_rs).wait_recv()

        @pl.when(inner)
        def _():
            for kv in range(4):
                relay_copy(g, kv, side_relay, side_recv, far_relay_ss, far_relay_rs).wait_recv()

    def back_start(g):
        mate_copy(g, back_send, back_recv, back_ss, back_rs).start()

        @pl.when(inner)
        def _():
            for kv in range(4):
                far_copy(g, kv, back_send, back_relay, farb_ss, farb_rs).start()

    def back_forward(g):
        @pl.when(outer)
        def _():
            for kv in range(4):
                far_copy(g, kv, back_send, back_relay, farb_ss, farb_rs).wait_recv()
                relay_copy(g, kv, back_relay, back_recv, farb_relay_ss, farb_relay_rs).start()

    def back_wait(g):
        mate_copy(g, back_send, back_recv, back_ss, back_rs).wait_recv()

        @pl.when(inner)
        def _():
            for kv in range(4):
                relay_copy(g, kv, back_relay, back_recv, farb_relay_ss, farb_relay_rs).wait_recv()

    def drain(g):
        mate_copy(g, side_send, side_recv, side_ss, side_rs).wait_send()
        mate_copy(g, back_send, back_recv, back_ss, back_rs).wait_send()

        @pl.when(inner)
        def _():
            for kv in range(4):
                far_copy(g, kv, side_send, side_relay, far_ss, far_rs).wait_send()
                far_copy(g, kv, back_send, back_relay, farb_ss, farb_rs).wait_send()

        @pl.when(outer)
        def _():
            for kv in range(4):
                relay_copy(g, kv, side_relay, side_recv, far_relay_ss, far_relay_rs).wait_send()
                relay_copy(g, kv, back_relay, back_recv, farb_relay_ss, farb_relay_rs).wait_send()

        for side in range(2):
            @pl.when(has_along[side])
            def _(side=side):
                rows_copy(g, side).wait_send()
                up_copy(g, side).wait_send()

    def up_copy(g, side):
        return remote(
            rows_send.at[g, side], rows_recv.at[g, side], up_ss.at[g, side], up_rs.at[g, side], along[side]
        )

    for g in range(4):
        for kv in range(2):
            loads[2 * g + kv].wait()
        for side in range(2):
            @pl.when(has_along[side])
            def _(g=g, side=side):
                rows_copy(g, side).start()

    for b in range(4):
        shape = (512, 128)
        key = lax.broadcasted_iota(jnp.int32, shape, 0)
        lane = lax.broadcasted_iota(jnp.int32, shape, 1) & 63
        key_row, slot = key >> 5, key & 31
        key_col = jnp.where(slot < 24, slot, slot - 30)
        down = key_row - (lane >> 4)
        aside = key_col - (lane & 15)
        grid_row = key_row + (gy * 16 + 4 * b - 6)
        grid_col = key_col + gx * 16
        allowed = (slot < 30) & (down >= 0) & (down <= 12) & (aside >= -6) & (aside <= 6)
        allowed = allowed & (grid_row >= 0) & (grid_row < 128) & (grid_col >= 0) & (grid_col < 64)
        half = jnp.where(allowed, 0.0, -1e30).astype(f32)
        bias[b] = jnp.concatenate([half, half], axis=1)

    def prepare(g):
        for side in range(2):
            zero_row = (22, 0)[side]

            @pl.when(has_along[side])
            def _(g=g, side=side):
                rows_copy(g, 1 - side).wait_recv()

            @pl.when(jnp.logical_not(has_along[side]))
            def _(g=g, zero_row=(0, 22)[side]):
                pad[g, :, zero_row : zero_row + 6, 0:16, :] = jnp.zeros((2, 6, 16, 256), bf16)

        tile_part = pad[g, :, :, 0:16, :].astype(f32)
        for piece in range(4):
            lanes = slice(128 * (piece % 2), 128 * (piece % 2) + 128)
            part = tile_part[piece // 2, :, :, lanes]
            for side, slab in ((0, part[:, 0:8]), (1, pltpu.roll(part[:, 8:16], 6, 1))):
                for n, packed in enumerate(pack_columns(slab)):
                    side_send[g, side, piece, :, n] = packed.astype(bf16)
        side_start(g)

    @pl.when(outer)
    def _():
        side_recv[:, pl.ds(1 - core, 1)] = jnp.zeros((4, 1, 4, 7, 3, 8, 128), bf16)
        back_recv[:, pl.ds(1 - core, 1)] = jnp.zeros((4, 1, 4, 7, 3, 8, 128), bf16)

    same_head = (lax.broadcasted_iota(jnp.int32, (256, 256), 0) >> 6) == (
        lax.broadcasted_iota(jnp.int32, (256, 256), 1) >> 6
    )
    head_mask = jnp.where(same_head, 1.0, 0.0).astype(bf16)

    def attend(g):
        columns = slice(256 * g, 256 * g + 256)
        acc[g] = jnp.zeros((2, 28, 32, 256), f32)

        def block(b, carry):
            keys = pad[g, 0, pl.ds(4 * b, 16)].reshape(512, 256)
            values = pad[g, 1, pl.ds(4 * b, 16)].reshape(512, 256)
            query = queries[b, :, columns] * jnp.asarray(0.125, bf16)
            grad = upstream[b, :, columns]
            query_heads = jnp.concatenate([query] * 4, axis=0) * head_mask
            grad_heads = jnp.concatenate([grad] * 4, axis=0) * head_mask
            scores = dot_nt(keys, query_heads) + bias[b]
            top = jnp.max(scores, axis=0, keepdims=True)
            exponent = jnp.exp(scores - top)
            total = jnp.sum(exponent, axis=0, keepdims=True)
            probs = exponent * (1.0 / total)
            probs_bf = probs.astype(bf16)
            grad_probs = dot_nt(values, grad_heads)
            centre = jnp.sum(probs * grad_probs, axis=0, keepdims=True)
            grad_scores = (probs * (grad_probs - centre)).astype(bf16)
            attended[b, :, columns] = head_diagonal(dot_tn(probs_bf, values)).astype(bf16)
            gproj[b, :, columns] = (head_diagonal(dot_tn(grad_scores, keys)) * 0.125).astype(bf16)
            rows = pl.ds(4 * b, 16)
            acc[g, 0, rows] += dot_nn(grad_scores, query_heads).reshape(16, 32, 256)
            acc[g, 1, rows] += dot_nn(probs_bf, grad_heads).reshape(16, 32, 256)
            return carry

        lax.fori_loop(0, 4, block, 0)

    def start_back(g):
        for piece in range(4):
            lanes = slice(128 * (piece % 2), 128 * (piece % 2) + 128)
            for side, lo in ((0, 24), (1, 16)):
                for n, packed in enumerate(pack_columns(acc[g, piece // 2, :, lo : lo + 8, lanes])):
                    back_send[g, side, piece, :, n] = packed.astype(bf16)
        back_start(g)

    def start_up(g):
        back_wait(g)
        place = lax.broadcasted_iota(jnp.int32, (28, 8, 128), 1)
        for piece in range(4):
            lanes = slice(128 * (piece % 2), 128 * (piece % 2) + 128)
            low, high = [
                jnp.where(
                    place < 6,
                    unpack_columns(*[back_recv[g, n, piece, :, m].astype(f32) for m in range(3)]),
                    0.0,
                )
                for n in (1, 0)
            ]
            acc[g, piece // 2, :, 0:8, lanes] += low
            acc[g, piece // 2, :, 8:16, lanes] += pltpu.roll(high, 2, 1)
        rows_send[g, 0] = acc[g, :, 0:6, 0:16, :].astype(bf16)
        rows_send[g, 1] = acc[g, :, 22:28, 0:16, :].astype(bf16)
        for side in range(2):
            @pl.when(has_along[side])
            def _(side=side):
                up_copy(g, side).start()

    def finish(g):
        for side in range(2):
            lo = (6, 16)[side]

            @pl.when(has_along[side])
            def _(side=side, lo=lo):
                up_copy(g, 1 - side).wait_recv()
                acc[g, :, lo : lo + 6, 0:16, :] += rows_recv[g, 1 - side].astype(f32)

        for kv in range(2):
            lo = 1024 * (kv + 1) + 256 * g
            gproj[:, :, lo : lo + 256] = acc[g, kv, 6:22, 0:16, :].reshape(4, 64, 256).astype(bf16)
            grad_swap(kv + 1, g)

    def unpack(g):
        side_wait(g)
        for piece in range(4):
            lanes = slice(128 * (piece % 2), 128 * (piece % 2) + 128)
            slabs = [
                unpack_columns(*[side_recv[g, n, piece, :, m].astype(f32) for m in range(3)]) for n in range(2)
            ]
            pad[g, piece // 2, :, 16:32, lanes] = jnp.concatenate(slabs, axis=1).astype(bf16)

    def grad_copy(j, g):
        lo = 1024 * j + 256 * g
        half = g % 2
        return remote(
            gproj.at[:, :, lo : lo + 256], b_mate.at[j, half], grad_ss.at[j, half], grad_rs.at[j, half], mate
        )

    def grad_swap(j, g):
        @pl.when(core != g // 2)
        def _():
            grad_copy(j, g).start()

    def left_copy(kind, n):
        return remote(
            at_own.at[kind, n], at_mate.at[kind, n], swap_ss.at[kind, n], swap_rs.at[kind, n], mate
        )

    branch_copies = []
    for half in range(2):
        lo = pl.multiple_of((1 - core) * 512 + 256 * half, 256)
        branch_copies.append(
            remote(branch.at[:, :, pl.ds(lo, 256)], b_mate.at[3, half], grad_ss.at[3, half], grad_rs.at[3, half], mate)
        )

    sbuf = [[ring_bufs[c * 3 + p] for p in range(3)] for c in range(4)]
    rbuf = [[ring_bufs[12 + c * 3 + p] for p in range(3)] for c in range(4)]
    keep = [[ring_bufs[24 + c * 3 + p] for p in range(3)] for c in range(4)]
    part = [[ring_bufs[36 + c * 3 + p] for p in range(3)] for c in range(4)]

    def ring_copy(c, p, s):
        by = 1 if s in (0, 2, 4) else -1
        return remote(
            sbuf[c][p].at[s], rbuf[c][p].at[s],
            ring_ss.at[c, p, s], ring_rs.at[c, p, s], neighbour(CHUNK_AXES[c][p], by),
        )

    def ring_block(c, p, by):
        axis = CHUNK_AXES[c][p]
        j = (axis_coord(axis) + by + 4) % 4
        if p > 0:
            return part[c][p - 1][pick(None, CHUNK_AXES[c][p:], axis, j)].reshape(256 >> (2 * p), 512)
        kind = 1 if c == 3 else 0
        index = (kind,) + pick(None, "xyz", axis, j)
        left_own = at_own[index].reshape(256, 256)
        left_mate = at_mate[index].reshape(256, 256)
        base = 0 if c == 3 else 1024 * c
        columns = pl.ds(pl.multiple_of(base + 512 * core, 512), 512)
        right_own = (branch if c == 3 else gproj)[:, :, columns].reshape(256, 512)
        right_mate = jnp.concatenate([b_mate[c, 0].reshape(256, 256), b_mate[c, 1].reshape(256, 256)], axis=1)
        return dot_nn(left_own, right_own) + dot_nn(left_mate, right_mate)

    def ring_start(c, p):
        value = ring_block(c, p, 2)
        sbuf[c][p][0] = value[:, :256].astype(bf16)
        ring_copy(c, p, 0).start()
        sbuf[c][p][1] = value[:, 256:].astype(bf16)
        ring_copy(c, p, 1).start()
        value = ring_block(c, p, 1)
        sbuf[c][p][2] = value[:, 256:].astype(bf16)
        ring_copy(c, p, 2).start()
        keep[c][p][0] = value[:, :256]
        value = ring_block(c, p, -1)
        sbuf[c][p][3] = value[:, :256].astype(bf16)
        ring_copy(c, p, 3).start()
        keep[c][p][1] = value[:, 256:]
        part[c][p][...] = ring_block(c, p, 0).reshape(part[c][p].shape)

    def ring_relay(c, p):
        for s in (0, 1):
            ring_copy(c, p, s).wait_recv()
            sbuf[c][p][4 + s] = (keep[c][p][s] + rbuf[c][p][s].astype(f32)).astype(bf16)
            ring_copy(c, p, 4 + s).start()

    def ring_finish(c, p):
        for s in (2, 3, 4, 5):
            ring_copy(c, p, s).wait_recv()
        shape = part[c][p].shape[:-1] + (256,)
        first = rbuf[c][p][3].astype(f32) + rbuf[c][p][4].astype(f32)
        second = rbuf[c][p][2].astype(f32) + rbuf[c][p][5].astype(f32)
        part[c][p][..., :256] += first.reshape(shape)
        part[c][p][..., 256:] += second.reshape(shape)

    def swap_wait(c):
        for half in range(2):
            grad_copy(c, half).wait_recv()

    def attend_all(g):
        unpack(g)
        attend(g)
        start_back(g)
        grad_swap(0, g)
        columns = slice(256 * g, 256 * g + 256)
        at_own[1, g] = attended[:, :, columns].reshape(256, 256).T.reshape(2, 4, 2, 16, 256)
        left_copy(1, g).start()

    for n in range(4):
        columns = slice(256 * n, 256 * n + 256)
        at_own[0, n] = normed[:, columns].T.reshape(2, 4, 2, 16, 256)
        left_copy(0, n).start()
    for copy in branch_copies:
        copy.start()
    prepare(0)
    prepare(1)
    side_forward(0)
    prepare(2)
    side_forward(1)
    query_load.wait()
    upstream_load.wait()
    attend_all(0)
    prepare(3)
    side_forward(2)
    attend_all(1)
    back_forward(0)
    side_forward(3)
    attend_all(2)
    back_forward(1)
    start_up(0)
    attend_all(3)
    back_forward(2)
    start_up(1)
    finish(0)
    for n in range(4):
        left_copy(0, n).wait_recv()
        left_copy(1, n).wait_recv()
    for copy in branch_copies:
        copy.wait_recv()
    swap_wait(0)
    ring_start(0, 0)
    back_forward(3)
    start_up(2)
    finish(1)
    ring_start(3, 0)
    start_up(3)
    finish(2)
    ring_relay(0, 0)
    finish(3)
    for c in (1, 2):
        swap_wait(c)
        ring_start(c, 0)
    ring_relay(3, 0)
    weight_load.wait()
    flat = attended[...].reshape(256, 1024)
    for n in range(4):
        columns = slice(256 * n, 256 * n + 256)
        product = dot_nn(flat, weight_vmem[:, 3072 + 256 * n : 3328 + 256 * n])
        block_output[:, columns] = (tokens[:, columns].astype(f32) + tissue[...] * product).astype(bf16)
    ring_relay(1, 0)
    ring_relay(2, 0)
    flat = gproj[...].reshape(256, 3072)
    for n in range(4):
        rows = slice(256 * n, 256 * n + 256)
        grad_normed[:, rows] = dot_nt(flat, weight_vmem[rows, 0:3072])
    for c in (0, 3, 1, 2):
        ring_finish(c, 0)
        ring_start(c, 1)
    for c in (0, 3, 1, 2):
        ring_relay(c, 1)

    def norm_rows(n, carry):
        rows = pl.ds(pl.multiple_of(64 * n, 64), 64)
        wide = tokens[rows, :].astype(f32)
        centred = wide - jnp.mean(wide, axis=1, keepdims=True)
        inverse = lax.rsqrt(jnp.mean(centred * centred, axis=1, keepdims=True) + EPSILON)
        normalized = centred * inverse
        scaled = grad_normed[rows, :] * gain[...]
        first_mean = jnp.mean(scaled, axis=1, keepdims=True)
        second_mean = jnp.mean(scaled * normalized, axis=1, keepdims=True)
        grad = cotangent[rows, :].astype(f32) + inverse * (scaled - first_mean - normalized * second_mean)
        input_grad[rows, :] = grad.astype(bf16)
        return carry

    lax.fori_loop(0, 4, norm_rows, 0)
    for c in (0, 3, 1, 2):
        ring_finish(c, 1)
        ring_start(c, 2)
    for c in (0, 3, 1, 2):
        ring_relay(c, 2)
    for c in (0, 3, 1, 2):
        ring_finish(c, 2)
        value = part[c][2][...] * inv_root
        mine = jnp.where(core == 0, value[:8], value[8:])
        theirs = jnp.where(core == 0, value[8:], value[:8])
        last_send[c] = theirs
        final_copy = remote(last_send.at[c], last_recv.at[c], swap_ss.at[2, c], swap_rs.at[2, c], mate)
        final_copy.start()
        offset = pl.multiple_of(1024 * c + 512 * core, 512)
        weight_grads[:, pl.ds(offset, 512)] = mine
    for c in (0, 3, 1, 2):
        final_copy = remote(last_send.at[c], last_recv.at[c], swap_ss.at[2, c], swap_rs.at[2, c], mate)
        final_copy.wait_recv()
        offset = pl.multiple_of(1024 * c + 512 * (1 - core), 512)
        weight_grads[:, pl.ds(offset, 512)] = last_recv[c]
        final_copy.wait_send()
        for p in range(3):
            for s in range(6):
                ring_copy(c, p, s).wait_send()
    for n in range(4):
        left_copy(0, n).wait_send()
        left_copy(1, n).wait_send()
        drain(n)
        for j in range(3):
            @pl.when(core != n // 2)
            def _(j=j, n=n):
                grad_copy(j, n).wait_send()
    for copy in branch_copies:
        copy.wait_send()


def sublayer(projected, grad_attn, weights, normed, branch, tokens, cotangent, tissue, gain, inv_root):
    bf16, f32 = jnp.bfloat16, jnp.float32
    dma = pltpu.SemaphoreType.DMA
    any_space = pl.BlockSpec(memory_space=pl.ANY)
    vmem = pl.BlockSpec(memory_space=pltpu.VMEM)
    ring = []
    for _ in range(2):
        for c in range(4):
            for p in range(3):
                ring.append(pltpu.VMEM((6, 256 >> (2 * p), 256), bf16))
    for c in range(4):
        for p in range(3):
            ring.append(pltpu.VMEM((2, 256 >> (2 * p), 256), f32))
    for c in range(4):
        for p in range(3):
            ring.append(pltpu.VMEM(row_dims(CHUNK_AXES[c][p + 1 :]) + (16, 512), f32))
    slab = pltpu.VMEM((4, 2, 4, 7, 3, 8, 128), bf16)
    relay = pltpu.VMEM((4, 4, 7, 3, 8, 128), bf16)
    return pl.pallas_call(
        functools.partial(sublayer_kernel, inv_root),
        out_shape=(
            jax.ShapeDtypeStruct((256, 1024), bf16),
            jax.ShapeDtypeStruct((256, 1024), bf16),
            jax.ShapeDtypeStruct((8, 4096), f32),
        ),
        in_specs=[any_space] * 4 + [vmem] * 6,
        out_specs=(vmem,) * 3,
        scratch_shapes=[
            pltpu.VMEM((4, 64, 1024), bf16),
            pltpu.VMEM((4, 64, 3072), bf16),
            pltpu.VMEM((1024, 4096), bf16),
            pltpu.VMEM((256, 1024), f32),
            pltpu.VMEM((4, 2, 28, 32, 256), bf16),
            pltpu.VMEM((4, 64, 1024), bf16),
            pltpu.VMEM((4, 64, 1024), bf16),
            pltpu.VMEM((4, 512, 256), f32),
            pltpu.VMEM((4, 2, 28, 32, 256), f32),
            slab, slab, slab, slab,
            pltpu.VMEM((4, 2, 2, 6, 16, 256), bf16),
            pltpu.VMEM((4, 2, 2, 6, 16, 256), bf16),
            relay, relay,
            pltpu.VMEM((2, 4, 2, 4, 2, 16, 256), bf16),
            pltpu.VMEM((2, 4, 2, 4, 2, 16, 256), bf16),
            pltpu.VMEM((4, 2, 4, 64, 256), bf16),
            pltpu.VMEM((4, 8, 512), f32),
            pltpu.VMEM((4, 8, 512), f32),
            dma((11,)),
        ]
        + [dma((4, 2))] * 4
        + [dma((4,))] * 4
        + [dma((4, 4))] * 8
        + [dma((3, 4))] * 2
        + [dma((4, 2))] * 2
        + [dma((4, 3, 6))] * 2
        + ring,
        compiler_params=pltpu.CompilerParams(
            collective_id=0, has_side_effects=True, vmem_limit_bytes=67043328
        ),
    )(
        projected.reshape(16, 16, 3072),
        projected.reshape(4, 64, 3072),
        grad_attn.reshape(4, 64, 1024),
        weights,
        normed,
        branch.reshape(4, 64, 1024),
        tokens,
        cotangent,
        tissue,
        gain,
    )


def local(tokens, weights, norm_gain, tissue, cotangent):
    model_width = tokens.shape[-1]
    token_count = tokens.shape[1] * tokens.shape[2]
    group_count = lax.axis_size("slide") * lax.axis_size("gy") * lax.axis_size("gx")
    inv_root = 1.0 / math.sqrt(group_count * token_count)
    weight_in = weights[:, : 3 * model_width]
    weight_out = weights[:, 3 * model_width :]
    tokens_float = tokens.reshape(token_count, model_width).astype(jnp.float32)
    row_mean = jnp.mean(tokens_float, axis=-1, keepdims=True)
    centered = tokens_float - row_mean
    variance = jnp.mean(centered * centered, axis=-1, keepdims=True)
    inverse = lax.rsqrt(variance + EPSILON)
    normalized = centered * inverse
    normed = (normalized * norm_gain).astype(jnp.bfloat16)
    projected = jnp.dot(normed, weight_in, preferred_element_type=jnp.float32).astype(jnp.bfloat16)
    tissue_mask = tissue.reshape(token_count, 1).astype(jnp.float32)
    upstream = cotangent.reshape(token_count, model_width).astype(jnp.float32)
    branch_grad = (tissue_mask * upstream).astype(jnp.bfloat16)
    grad_attn = jnp.dot(branch_grad, weight_out.T, preferred_element_type=jnp.float32).astype(
        jnp.bfloat16
    )
    block_output, input_grad, weight_grads = sublayer(
        projected,
        grad_attn,
        weights,
        normed,
        branch_grad,
        tokens.reshape(token_count, model_width),
        cotangent.reshape(token_count, model_width),
        tissue_mask,
        norm_gain.reshape(1, model_width),
        inv_root,
    )
    return (block_output.reshape(tokens.shape), input_grad.reshape(tokens.shape), weight_grads)


def solution(mesh):
    in_specs = (
        P("slide", "gy", "gx", None),
        P(),
        P(),
        P("slide", "gy", "gx"),
        P("slide", "gy", "gx", None),
    )
    out_specs = (
        P("slide", "gy", "gx", None),
        P("slide", "gy", "gx", None),
        P(("slide", "gy", "gx"), None),
    )
    return jax.shard_map(local, mesh=mesh, in_specs=in_specs, out_specs=out_specs, check_vma=False)
```

```python
import functools
import math

import jax
import jax.numpy as jnp
from jax import lax
from jax.experimental import pallas as pl
from jax.experimental.pallas import tpu as pltpu
from jax.sharding import PartitionSpec as P

EPSILON = 1e-06


LOADED_UP = 0
LOADED_DOWN = 3
CHUNK_AXES = ("xyz", "yzx", "zxy", "xzy")


def coords():
    x = lax.axis_index("slide")
    gy = lax.axis_index("gy")
    gx = lax.axis_index("gx")
    zlo, y = gy // 4, gy % 4
    zhi, core = gx // 2, gx % 2
    return x, y, zhi * 2 + zlo, core


def device_at(x, y, z, core):
    return (x, (z % 2) * 4 + y, (z // 2) * 2 + core)


def neighbour(axis, by):
    x, y, z, core = coords()
    if axis == "x":
        return device_at((x + by + 4) % 4, y, z, core)
    if axis == "y":
        return device_at(x, (y + by + 4) % 4, z, core)
    return device_at(x, y, (z + by + 4) % 4, core)


def mate_id():
    x, y, z, core = coords()
    return device_at(x, y, z, 1 - core)


def axis_coord(axis):
    x, y, z, _ = coords()
    return {"x": x, "y": y, "z": z}[axis]


def pick(ref, left, axis, j):
    dims = [d for d in ("x", "l", "y", "h") if (d in left) or (d in "lh" and "z" in left)]
    index = []
    for d in dims:
        if d == axis:
            index.append(j)
        elif axis == "z" and d == "l":
            index.append(j % 2)
        elif axis == "z" and d == "h":
            index.append(j // 2)
        else:
            index.append(slice(None))
    return tuple(index)


def row_dims(left):
    out = []
    if "x" in left:
        out.append(4)
    if "z" in left:
        out.append(2)
    if "y" in left:
        out.append(4)
    if "z" in left:
        out.append(2)
    return tuple(out)


def remote(src, dst, ssem, rsem, dev):
    return pltpu.make_async_remote_copy(
        src_ref=src, dst_ref=dst, send_sem=ssem, recv_sem=rsem,
        device_id=dev, device_id_type=pl.DeviceIdType.MESH,
    )


def dot_nn(left, right):
    return jnp.dot(left, right, preferred_element_type=jnp.float32)


def dot_nt(left, right):
    return lax.dot_general(left, right, (((1,), (1,)), ((), ())), preferred_element_type=jnp.float32)


def dot_tn(left, right):
    return lax.dot_general(left, right, (((0,), (0,)), ((), ())), preferred_element_type=jnp.float32)


def head_diagonal(full):
    low = lax.broadcasted_iota(jnp.int32, (64, 128), 1) < 64
    first = jnp.where(low, full[0:64, 0:128], full[64:128, 0:128])
    second = jnp.where(low, full[128:192, 128:256], full[192:256, 128:256])
    return jnp.concatenate([first, second], axis=1)


def pack_columns(slab):
    parts = slab.reshape(7, 4, 8, 128)
    place = lax.broadcasted_iota(jnp.int32, (7, 8, 128), 1)
    one = pltpu.roll(parts[:, 1], 6, 1)
    two = pltpu.roll(parts[:, 2], 4, 1)
    three = pltpu.roll(parts[:, 3], 2, 1)
    return (
        jnp.where(place < 6, parts[:, 0], one),
        jnp.where(place < 4, one, two),
        jnp.where(place < 2, two, three),
    )


def unpack_columns(first, second, third):
    place = lax.broadcasted_iota(jnp.int32, (7, 8, 128), 1)
    rows = (
        first,
        pltpu.roll(jnp.where(place < 4, second, first), 2, 1),
        pltpu.roll(jnp.where(place < 2, third, second), 4, 1),
        pltpu.roll(third, 6, 1),
    )
    return jnp.stack(rows, axis=1).reshape(28, 8, 128)


def sublayer_kernel(
    inv_root,
    weights, tokens, cotangent, tissue, gain,
    block_output, input_grad, weight_grads,
    normed, branch, mask, attended, gproj, weight_vmem, grad_normed,
    pad, queries, upstream, bias, acc,
    side_send, side_recv, back_send, back_recv, rows_send, rows_recv, side_relay, back_relay,
    at_own, at_mate, b_mate, last_send, last_recv,
    load_sem, rows_ss, rows_rs, up_ss, up_rs, side_ss, side_rs, back_ss, back_rs,
    far_ss, far_rs, far_relay_ss, far_relay_rs, farb_ss, farb_rs, farb_relay_ss, farb_relay_rs,
    swap_ss, swap_rs, grad_ss, grad_rs, ring_ss, ring_rs,
    *ring_bufs,
):
    f32, bf16 = jnp.float32, jnp.bfloat16
    slide = lax.axis_index("slide")
    gy = lax.axis_index("gy")
    gx = lax.axis_index("gx")
    _, y, z, core = coords()
    along = ((slide, gy - 1, gx), (slide, gy + 1, gx))
    has_along = (gy > 0, gy < 7)
    outer = (gx == 0) | (gx == 3)
    inner = jnp.logical_not(outer)
    mate = mate_id()
    signs = (1, jnp.where(y == LOADED_UP, -1, 1), jnp.where(y == LOADED_DOWN, 1, -1), -1)

    def opposite(by):
        other = (z + by + 4) % 4
        high = other // 2
        return (slide, (other % 2) * 4 + y, jnp.where(outer, high + 1, 3 * high))

    across = [opposite(sign) for sign in signs]

    loads = []
    for g in range(4):
        for kv in range(2):
            columns = slice(1024 * (kv + 1) + 256 * g, 1024 * (kv + 1) + 256 * g + 256)
            loads.append(
                pltpu.make_async_copy(
                    weights.at[:, columns], weight_vmem.at[:, columns], load_sem.at[2 * g + kv]
                )
            )
    for n, columns in ((8, slice(0, 1024)), (9, slice(3072, 4096))):
        loads.append(
            pltpu.make_async_copy(weights.at[:, columns], weight_vmem.at[:, columns], load_sem.at[n])
        )
    for load in loads:
        load.start()

    barrier = pltpu.get_barrier_semaphore()
    greeted = [mate, (slide, (gy + 7) % 8, gx), (slide, (gy + 1) % 8, gx), opposite(1), opposite(-1)]
    greeted += [neighbour(axis, by) for axis in "xyz" for by in (1, -1)]
    for dev in greeted:
        pl.semaphore_signal(barrier, inc=1, device_id=dev, device_id_type=pl.DeviceIdType.MESH)
    flags = tissue[...].astype(f32)
    place = lax.broadcasted_iota(jnp.int32, (16, 16, 16), 1) == lax.broadcasted_iota(jnp.int32, (16, 16, 16), 2)
    picked = jnp.where(place, jnp.broadcast_to(flags[:, None, :], (16, 16, 16)), 0.0)
    mask[...] = jnp.sum(picked, axis=2, keepdims=True).reshape(256, 1)

    def norm_forward(n, carry):
        rows = pl.ds(pl.multiple_of(64 * n, 64), 64)
        wide = tokens[rows, :].astype(f32)
        centred = wide - jnp.mean(wide, axis=1, keepdims=True)
        inverse = lax.rsqrt(jnp.mean(centred * centred, axis=1, keepdims=True) + EPSILON)
        normed[rows, :] = (centred * inverse * gain[...]).astype(bf16)
        branch[n] = (mask[rows, :] * cotangent[rows, :].astype(f32)).astype(bf16)
        return carry

    lax.fori_loop(0, 4, norm_forward, 0)
    pl.semaphore_wait(barrier, len(greeted))

    def rows_copy(g, side):
        src = (6, 16)[side]
        dst = (22, 0)[side]
        return remote(
            pad.at[g, :, src : src + 6, 0:16, :], pad.at[g, :, dst : dst + 6, 0:16, :],
            rows_ss.at[g, side], rows_rs.at[g, side], along[side],
        )

    def mate_copy(g, sent, got, ss, rs):
        return remote(sent.at[g, 1 - core], got.at[g, 1 - core], ss.at[g], rs.at[g], mate)

    def far_copy(g, kv, sent, relay, ss, rs):
        return remote(sent.at[g, core, kv], relay.at[g, kv], ss.at[g, kv], rs.at[g, kv], across[kv])

    def relay_copy(g, kv, relay, got, ss, rs):
        source = (z - signs[kv] + 4) % 4
        return remote(
            relay.at[g, kv], got.at[g, 1 - source // 2, kv], ss.at[g, kv], rs.at[g, kv], across[kv]
        )

    def side_start(g):
        mate_copy(g, side_send, side_recv, side_ss, side_rs).start()

        @pl.when(inner)
        def _():
            for kv in range(4):
                far_copy(g, kv, side_send, side_relay, far_ss, far_rs).start()

    def side_forward(g):
        @pl.when(outer)
        def _():
            for kv in range(4):
                far_copy(g, kv, side_send, side_relay, far_ss, far_rs).wait_recv()
                relay_copy(g, kv, side_relay, side_recv, far_relay_ss, far_relay_rs).start()

    def side_wait(g):
        mate_copy(g, side_send, side_recv, side_ss, side_rs).wait_recv()

        @pl.when(inner)
        def _():
            for kv in range(4):
                relay_copy(g, kv, side_relay, side_recv, far_relay_ss, far_relay_rs).wait_recv()

    def back_start(g):
        mate_copy(g, back_send, back_recv, back_ss, back_rs).start()

        @pl.when(inner)
        def _():
            for kv in range(4):
                far_copy(g, kv, back_send, back_relay, farb_ss, farb_rs).start()

    def back_forward(g):
        @pl.when(outer)
        def _():
            for kv in range(4):
                far_copy(g, kv, back_send, back_relay, farb_ss, farb_rs).wait_recv()
                relay_copy(g, kv, back_relay, back_recv, farb_relay_ss, farb_relay_rs).start()

    def back_wait(g):
        mate_copy(g, back_send, back_recv, back_ss, back_rs).wait_recv()

        @pl.when(inner)
        def _():
            for kv in range(4):
                relay_copy(g, kv, back_relay, back_recv, farb_relay_ss, farb_relay_rs).wait_recv()

    def drain(g):
        mate_copy(g, side_send, side_recv, side_ss, side_rs).wait_send()
        mate_copy(g, back_send, back_recv, back_ss, back_rs).wait_send()

        @pl.when(inner)
        def _():
            for kv in range(4):
                far_copy(g, kv, side_send, side_relay, far_ss, far_rs).wait_send()
                far_copy(g, kv, back_send, back_relay, farb_ss, farb_rs).wait_send()

        @pl.when(outer)
        def _():
            for kv in range(4):
                relay_copy(g, kv, side_relay, side_recv, far_relay_ss, far_relay_rs).wait_send()
                relay_copy(g, kv, back_relay, back_recv, farb_relay_ss, farb_relay_rs).wait_send()

        for side in range(2):
            @pl.when(has_along[side])
            def _(side=side):
                rows_copy(g, side).wait_send()
                up_copy(g, side).wait_send()

    def up_copy(g, side):
        return remote(
            rows_send.at[g, side], rows_recv.at[g, side], up_ss.at[g, side], up_rs.at[g, side], along[side]
        )

    for g in range(4):
        for kv in range(2):
            loads[2 * g + kv].wait()
            columns = slice(1024 * (kv + 1) + 256 * g, 1024 * (kv + 1) + 256 * g + 256)
            made = dot_nn(normed[...], weight_vmem[:, columns]).astype(bf16)
            pad[g, kv, 6:22, 0:16, :] = made.reshape(16, 16, 256)
        for side in range(2):
            @pl.when(has_along[side])
            def _(g=g, side=side):
                rows_copy(g, side).start()

    for b in range(4):
        shape = (512, 128)
        key = lax.broadcasted_iota(jnp.int32, shape, 0)
        lane = lax.broadcasted_iota(jnp.int32, shape, 1) & 63
        key_row, slot = key >> 5, key & 31
        key_col = jnp.where(slot < 24, slot, slot - 30)
        down = key_row - (lane >> 4)
        aside = key_col - (lane & 15)
        grid_row = key_row + (gy * 16 + 4 * b - 6)
        grid_col = key_col + gx * 16
        allowed = (slot < 30) & (down >= 0) & (down <= 12) & (aside >= -6) & (aside <= 6)
        allowed = allowed & (grid_row >= 0) & (grid_row < 128) & (grid_col >= 0) & (grid_col < 64)
        half = jnp.where(allowed, 0.0, -1e30).astype(f32)
        bias[b] = jnp.concatenate([half, half], axis=1)

    def prepare(g):
        for side in range(2):
            zero_row = (22, 0)[side]

            @pl.when(has_along[side])
            def _(g=g, side=side):
                rows_copy(g, 1 - side).wait_recv()

            @pl.when(jnp.logical_not(has_along[side]))
            def _(g=g, zero_row=(0, 22)[side]):
                pad[g, :, zero_row : zero_row + 6, 0:16, :] = jnp.zeros((2, 6, 16, 256), bf16)

        tile_part = pad[g, :, :, 0:16, :].astype(f32)
        for piece in range(4):
            lanes = slice(128 * (piece % 2), 128 * (piece % 2) + 128)
            part = tile_part[piece // 2, :, :, lanes]
            for side, slab in ((0, part[:, 0:8]), (1, pltpu.roll(part[:, 8:16], 6, 1))):
                for n, packed in enumerate(pack_columns(slab)):
                    side_send[g, side, piece, :, n] = packed.astype(bf16)
        side_start(g)

    @pl.when(outer)
    def _():
        side_recv[:, pl.ds(1 - core, 1)] = jnp.zeros((4, 1, 4, 7, 3, 8, 128), bf16)
        back_recv[:, pl.ds(1 - core, 1)] = jnp.zeros((4, 1, 4, 7, 3, 8, 128), bf16)

    same_head = (lax.broadcasted_iota(jnp.int32, (256, 256), 0) >> 6) == (
        lax.broadcasted_iota(jnp.int32, (256, 256), 1) >> 6
    )
    head_mask = jnp.where(same_head, 1.0, 0.0).astype(bf16)

    def attend(g):
        columns = slice(256 * g, 256 * g + 256)
        acc[g] = jnp.zeros((2, 28, 32, 256), f32)

        def block(b, carry):
            keys = pad[g, 0, pl.ds(4 * b, 16)].reshape(512, 256)
            values = pad[g, 1, pl.ds(4 * b, 16)].reshape(512, 256)
            query = queries[b, :, columns]
            grad = upstream[b, :, columns]
            query_heads = jnp.concatenate([query] * 4, axis=0) * head_mask
            grad_heads = jnp.concatenate([grad] * 4, axis=0) * head_mask
            scores = dot_nt(keys, query_heads) + bias[b]
            top = jnp.max(scores, axis=0, keepdims=True)
            exponent = jnp.exp(scores - top)
            total = jnp.sum(exponent, axis=0, keepdims=True)
            probs = exponent * (1.0 / total)
            probs_bf = probs.astype(bf16)
            grad_probs = dot_nt(values, grad_heads)
            centre = jnp.sum(probs * grad_probs, axis=0, keepdims=True)
            grad_scores = (probs * (grad_probs - centre)).astype(bf16)
            attended[b, :, columns] = head_diagonal(dot_tn(probs_bf, values)).astype(bf16)
            gproj[b, :, columns] = (head_diagonal(dot_tn(grad_scores, keys)) * 0.125).astype(bf16)
            rows = pl.ds(4 * b, 16)
            acc[g, 0, rows] += dot_nn(grad_scores, query_heads).reshape(16, 32, 256)
            acc[g, 1, rows] += dot_nn(probs_bf, grad_heads).reshape(16, 32, 256)
            return carry

        lax.fori_loop(0, 4, block, 0)

    def start_back(g):
        for piece in range(4):
            lanes = slice(128 * (piece % 2), 128 * (piece % 2) + 128)
            for side, lo in ((0, 24), (1, 16)):
                for n, packed in enumerate(pack_columns(acc[g, piece // 2, :, lo : lo + 8, lanes])):
                    back_send[g, side, piece, :, n] = packed.astype(bf16)
        back_start(g)

    def start_up(g):
        back_wait(g)
        place = lax.broadcasted_iota(jnp.int32, (28, 8, 128), 1)
        for piece in range(4):
            lanes = slice(128 * (piece % 2), 128 * (piece % 2) + 128)
            low, high = [
                jnp.where(
                    place < 6,
                    unpack_columns(*[back_recv[g, n, piece, :, m].astype(f32) for m in range(3)]),
                    0.0,
                )
                for n in (1, 0)
            ]
            acc[g, piece // 2, :, 0:8, lanes] += low
            acc[g, piece // 2, :, 8:16, lanes] += pltpu.roll(high, 2, 1)
        rows_send[g, 0] = acc[g, :, 0:6, 0:16, :].astype(bf16)
        rows_send[g, 1] = acc[g, :, 22:28, 0:16, :].astype(bf16)
        for side in range(2):
            @pl.when(has_along[side])
            def _(side=side):
                up_copy(g, side).start()

    def finish(g):
        for side in range(2):
            lo = (6, 16)[side]

            @pl.when(has_along[side])
            def _(side=side, lo=lo):
                up_copy(g, 1 - side).wait_recv()
                acc[g, :, lo : lo + 6, 0:16, :] += rows_recv[g, 1 - side].astype(f32)

        for kv in range(2):
            lo = 1024 * (kv + 1) + 256 * g
            gproj[:, :, lo : lo + 256] = acc[g, kv, 6:22, 0:16, :].reshape(4, 64, 256).astype(bf16)
            grad_swap(kv + 1, g)

    def unpack(g):
        side_wait(g)
        for piece in range(4):
            lanes = slice(128 * (piece % 2), 128 * (piece % 2) + 128)
            slabs = [
                unpack_columns(*[side_recv[g, n, piece, :, m].astype(f32) for m in range(3)]) for n in range(2)
            ]
            pad[g, piece // 2, :, 16:32, lanes] = jnp.concatenate(slabs, axis=1).astype(bf16)

    def grad_copy(j, g):
        lo = 1024 * j + 256 * g
        half = g % 2
        return remote(
            gproj.at[:, :, lo : lo + 256], b_mate.at[j, half], grad_ss.at[j, half], grad_rs.at[j, half], mate
        )

    def grad_swap(j, g):
        @pl.when(core != g // 2)
        def _():
            grad_copy(j, g).start()

    def left_copy(kind, n):
        return remote(
            at_own.at[kind, n], at_mate.at[kind, n], swap_ss.at[kind, n], swap_rs.at[kind, n], mate
        )

    branch_copies = []
    for half in range(2):
        lo = pl.multiple_of((1 - core) * 512 + 256 * half, 256)
        branch_copies.append(
            remote(branch.at[:, :, pl.ds(lo, 256)], b_mate.at[3, half], grad_ss.at[3, half], grad_rs.at[3, half], mate)
        )

    sbuf = [[ring_bufs[c * 3 + p] for p in range(3)] for c in range(4)]
    rbuf = [[ring_bufs[12 + c * 3 + p] for p in range(3)] for c in range(4)]
    keep = [[ring_bufs[24 + c * 3 + p] for p in range(3)] for c in range(4)]
    part = [[ring_bufs[36 + c * 3 + p] for p in range(3)] for c in range(4)]

    def ring_copy(c, p, s):
        by = 1 if s in (0, 2, 4) else -1
        return remote(
            sbuf[c][p].at[s], rbuf[c][p].at[s],
            ring_ss.at[c, p, s], ring_rs.at[c, p, s], neighbour(CHUNK_AXES[c][p], by),
        )

    def ring_block(c, p, by):
        axis = CHUNK_AXES[c][p]
        j = (axis_coord(axis) + by + 4) % 4
        if p > 0:
            return part[c][p - 1][pick(None, CHUNK_AXES[c][p:], axis, j)].reshape(256 >> (2 * p), 512)
        kind = 1 if c == 3 else 0
        index = (kind,) + pick(None, "xyz", axis, j)
        left_own = at_own[index].reshape(256, 256)
        left_mate = at_mate[index].reshape(256, 256)
        base = 0 if c == 3 else 1024 * c
        columns = pl.ds(pl.multiple_of(base + 512 * core, 512), 512)
        right_own = (branch if c == 3 else gproj)[:, :, columns].reshape(256, 512)
        right_mate = jnp.concatenate([b_mate[c, 0].reshape(256, 256), b_mate[c, 1].reshape(256, 256)], axis=1)
        return dot_nn(left_own, right_own) + dot_nn(left_mate, right_mate)

    def ring_start(c, p):
        value = ring_block(c, p, 2)
        sbuf[c][p][0] = value[:, :256].astype(bf16)
        ring_copy(c, p, 0).start()
        sbuf[c][p][1] = value[:, 256:].astype(bf16)
        ring_copy(c, p, 1).start()
        value = ring_block(c, p, 1)
        sbuf[c][p][2] = value[:, 256:].astype(bf16)
        ring_copy(c, p, 2).start()
        keep[c][p][0] = value[:, :256]
        value = ring_block(c, p, -1)
        sbuf[c][p][3] = value[:, :256].astype(bf16)
        ring_copy(c, p, 3).start()
        keep[c][p][1] = value[:, 256:]
        part[c][p][...] = ring_block(c, p, 0).reshape(part[c][p].shape)

    def ring_relay(c, p):
        for s in (0, 1):
            ring_copy(c, p, s).wait_recv()
            sbuf[c][p][4 + s] = (keep[c][p][s] + rbuf[c][p][s].astype(f32)).astype(bf16)
            ring_copy(c, p, 4 + s).start()

    def ring_finish(c, p):
        for s in (2, 3, 4, 5):
            ring_copy(c, p, s).wait_recv()
        shape = part[c][p].shape[:-1] + (256,)
        first = rbuf[c][p][3].astype(f32) + rbuf[c][p][4].astype(f32)
        second = rbuf[c][p][2].astype(f32) + rbuf[c][p][5].astype(f32)
        part[c][p][..., :256] += first.reshape(shape)
        part[c][p][..., 256:] += second.reshape(shape)

    def swap_wait(c):
        for half in range(2):
            grad_copy(c, half).wait_recv()

    def attend_all(g):
        unpack(g)
        attend(g)
        start_back(g)
        grad_swap(0, g)
        columns = slice(256 * g, 256 * g + 256)
        at_own[1, g] = attended[:, :, columns].reshape(256, 256).T.reshape(2, 4, 2, 16, 256)
        left_copy(1, g).start()

    for n in range(4):
        columns = slice(256 * n, 256 * n + 256)
        at_own[0, n] = normed[:, columns].T.reshape(2, 4, 2, 16, 256)
        left_copy(0, n).start()
    for copy in branch_copies:
        copy.start()
    loads[8].wait()
    for n in range(4):
        columns = slice(256 * n, 256 * n + 256)
        made = dot_nn(normed[...], weight_vmem[:, columns]).astype(bf16) * jnp.asarray(0.125, bf16)
        queries[:, :, columns] = made.reshape(4, 64, 256)
    loads[9].wait()
    flat = branch[...].reshape(256, 1024)
    for n in range(4):
        columns = slice(256 * n, 256 * n + 256)
        made = dot_nt(flat, weight_vmem[columns, 3072:4096]).astype(bf16)
        upstream[:, :, columns] = made.reshape(4, 64, 256)
    prepare(0)
    prepare(1)
    side_forward(0)
    prepare(2)
    side_forward(1)
    attend_all(0)
    prepare(3)
    side_forward(2)
    attend_all(1)
    back_forward(0)
    side_forward(3)
    attend_all(2)
    back_forward(1)
    start_up(0)
    attend_all(3)
    back_forward(2)
    start_up(1)
    finish(0)
    for n in range(4):
        left_copy(0, n).wait_recv()
        left_copy(1, n).wait_recv()
    for copy in branch_copies:
        copy.wait_recv()
    swap_wait(0)
    ring_start(0, 0)
    back_forward(3)
    start_up(2)
    finish(1)
    ring_start(3, 0)
    start_up(3)
    finish(2)
    ring_relay(0, 0)
    finish(3)
    for c in (1, 2):
        swap_wait(c)
        ring_start(c, 0)
    ring_relay(3, 0)
    flat = attended[...].reshape(256, 1024)
    for n in range(4):
        columns = slice(256 * n, 256 * n + 256)
        product = dot_nn(flat, weight_vmem[:, 3072 + 256 * n : 3328 + 256 * n])
        block_output[:, columns] = (tokens[:, columns].astype(f32) + mask[...] * product).astype(bf16)
    ring_relay(1, 0)
    ring_relay(2, 0)
    flat = gproj[...].reshape(256, 3072)
    for n in range(4):
        rows = slice(256 * n, 256 * n + 256)
        grad_normed[:, rows] = dot_nt(flat, weight_vmem[rows, 0:3072])
    for c in (0, 3, 1, 2):
        ring_finish(c, 0)
        ring_start(c, 1)
    for c in (0, 3, 1, 2):
        ring_relay(c, 1)

    def norm_rows(n, carry):
        rows = pl.ds(pl.multiple_of(64 * n, 64), 64)
        wide = tokens[rows, :].astype(f32)
        centred = wide - jnp.mean(wide, axis=1, keepdims=True)
        inverse = lax.rsqrt(jnp.mean(centred * centred, axis=1, keepdims=True) + EPSILON)
        normalized = centred * inverse
        scaled = grad_normed[rows, :] * gain[...]
        first_mean = jnp.mean(scaled, axis=1, keepdims=True)
        second_mean = jnp.mean(scaled * normalized, axis=1, keepdims=True)
        grad = cotangent[rows, :].astype(f32) + inverse * (scaled - first_mean - normalized * second_mean)
        input_grad[rows, :] = grad.astype(bf16)
        return carry

    lax.fori_loop(0, 4, norm_rows, 0)
    for c in (0, 3, 1, 2):
        ring_finish(c, 1)
        ring_start(c, 2)
    for c in (0, 3, 1, 2):
        ring_relay(c, 2)
    for c in (0, 3, 1, 2):
        ring_finish(c, 2)
        value = part[c][2][...] * inv_root
        mine = jnp.where(core == 0, value[:8], value[8:])
        theirs = jnp.where(core == 0, value[8:], value[:8])
        last_send[c] = theirs
        final_copy = remote(last_send.at[c], last_recv.at[c], swap_ss.at[2, c], swap_rs.at[2, c], mate)
        final_copy.start()
        offset = pl.multiple_of(1024 * c + 512 * core, 512)
        weight_grads[:, pl.ds(offset, 512)] = mine
    for c in (0, 3, 1, 2):
        final_copy = remote(last_send.at[c], last_recv.at[c], swap_ss.at[2, c], swap_rs.at[2, c], mate)
        final_copy.wait_recv()
        offset = pl.multiple_of(1024 * c + 512 * (1 - core), 512)
        weight_grads[:, pl.ds(offset, 512)] = last_recv[c]
        final_copy.wait_send()
        for p in range(3):
            for s in range(6):
                ring_copy(c, p, s).wait_send()
    for n in range(4):
        left_copy(0, n).wait_send()
        left_copy(1, n).wait_send()
        drain(n)
        for j in range(3):
            @pl.when(core != n // 2)
            def _(j=j, n=n):
                grad_copy(j, n).wait_send()
    for copy in branch_copies:
        copy.wait_send()


def sublayer(weights, tokens, cotangent, tissue, gain, inv_root):
    bf16, f32 = jnp.bfloat16, jnp.float32
    dma = pltpu.SemaphoreType.DMA
    any_space = pl.BlockSpec(memory_space=pl.ANY)
    vmem = pl.BlockSpec(memory_space=pltpu.VMEM)
    ring = []
    for _ in range(2):
        for c in range(4):
            for p in range(3):
                ring.append(pltpu.VMEM((6, 256 >> (2 * p), 256), bf16))
    for c in range(4):
        for p in range(3):
            ring.append(pltpu.VMEM((2, 256 >> (2 * p), 256), f32))
    for c in range(4):
        for p in range(3):
            ring.append(pltpu.VMEM(row_dims(CHUNK_AXES[c][p + 1 :]) + (16, 512), f32))
    slab = pltpu.VMEM((4, 2, 4, 7, 3, 8, 128), bf16)
    relay = pltpu.VMEM((4, 4, 7, 3, 8, 128), bf16)
    return pl.pallas_call(
        functools.partial(sublayer_kernel, inv_root),
        out_shape=(
            jax.ShapeDtypeStruct((256, 1024), bf16),
            jax.ShapeDtypeStruct((256, 1024), bf16),
            jax.ShapeDtypeStruct((8, 4096), f32),
        ),
        in_specs=[any_space] + [vmem] * 4,
        out_specs=(vmem,) * 3,
        scratch_shapes=[
            pltpu.VMEM((256, 1024), bf16),
            pltpu.VMEM((4, 64, 1024), bf16),
            pltpu.VMEM((256, 1), f32),
            pltpu.VMEM((4, 64, 1024), bf16),
            pltpu.VMEM((4, 64, 3072), bf16),
            pltpu.VMEM((1024, 4096), bf16),
            pltpu.VMEM((256, 1024), f32),
            pltpu.VMEM((4, 2, 28, 32, 256), bf16),
            pltpu.VMEM((4, 64, 1024), bf16),
            pltpu.VMEM((4, 64, 1024), bf16),
            pltpu.VMEM((4, 512, 256), f32),
            pltpu.VMEM((4, 2, 28, 32, 256), f32),
            slab, slab, slab, slab,
            pltpu.VMEM((4, 2, 2, 6, 16, 256), bf16),
            pltpu.VMEM((4, 2, 2, 6, 16, 256), bf16),
            relay, relay,
            pltpu.VMEM((2, 4, 2, 4, 2, 16, 256), bf16),
            pltpu.VMEM((2, 4, 2, 4, 2, 16, 256), bf16),
            pltpu.VMEM((4, 2, 4, 64, 256), bf16),
            pltpu.VMEM((4, 8, 512), f32),
            pltpu.VMEM((4, 8, 512), f32),
            dma((10,)),
        ]
        + [dma((4, 2))] * 4
        + [dma((4,))] * 4
        + [dma((4, 4))] * 8
        + [dma((3, 4))] * 2
        + [dma((4, 2))] * 2
        + [dma((4, 3, 6))] * 2
        + ring,
        compiler_params=pltpu.CompilerParams(
            collective_id=0, has_side_effects=True, vmem_limit_bytes=67043328
        ),
    )(weights, tokens, cotangent, tissue, gain)


def local(tokens, weights, norm_gain, tissue, cotangent):
    model_width = tokens.shape[-1]
    token_count = tokens.shape[1] * tokens.shape[2]
    group_count = lax.axis_size("slide") * lax.axis_size("gy") * lax.axis_size("gx")
    inv_root = 1.0 / math.sqrt(group_count * token_count)
    block_output, input_grad, weight_grads = sublayer(
        weights,
        tokens.reshape(token_count, model_width),
        cotangent.reshape(token_count, model_width),
        tissue[0],
        norm_gain.reshape(1, model_width),
        inv_root,
    )
    return (block_output.reshape(tokens.shape), input_grad.reshape(tokens.shape), weight_grads)


def solution(mesh):
    in_specs = (
        P("slide", "gy", "gx", None),
        P(),
        P(),
        P("slide", "gy", "gx"),
        P("slide", "gy", "gx", None),
    )
    out_specs = (
        P("slide", "gy", "gx", None),
        P("slide", "gy", "gx", None),
        P(("slide", "gy", "gx"), None),
    )
    return jax.shard_map(local, mesh=mesh, in_specs=in_specs, out_specs=out_specs, check_vma=False)
```

```python
import functools
import math

import jax
import jax.numpy as jnp
from jax import lax
from jax.experimental import pallas as pl
from jax.experimental.pallas import tpu as pltpu
from jax.sharding import PartitionSpec as P

EPSILON = 1e-06


DIRECT_FROM = 1
CHUNK_AXES = ("xyz", "yzx", "xzy", "zyx")


def coords():
    x = lax.axis_index("slide")
    gy = lax.axis_index("gy")
    gx = lax.axis_index("gx")
    zlo, y = gy // 4, gy % 4
    zhi, core = gx // 2, gx % 2
    return x, y, zhi * 2 + zlo, core


def device_at(x, y, z, core):
    return (x, (z % 2) * 4 + y, (z // 2) * 2 + core)


def neighbour(axis, by):
    x, y, z, core = coords()
    if axis == "x":
        return device_at((x + by + 4) % 4, y, z, core)
    if axis == "y":
        return device_at(x, (y + by + 4) % 4, z, core)
    return device_at(x, y, (z + by + 4) % 4, core)


def mate_id():
    x, y, z, core = coords()
    return device_at(x, y, z, 1 - core)


def axis_coord(axis):
    x, y, z, _ = coords()
    return {"x": x, "y": y, "z": z}[axis]


def pick(ref, left, axis, j):
    dims = [d for d in ("x", "l", "y", "h") if (d in left) or (d in "lh" and "z" in left)]
    index = []
    for d in dims:
        if d == axis:
            index.append(j)
        elif axis == "z" and d == "l":
            index.append(j % 2)
        elif axis == "z" and d == "h":
            index.append(j // 2)
        else:
            index.append(slice(None))
    return tuple(index)


def row_dims(left):
    out = []
    if "x" in left:
        out.append(4)
    if "z" in left:
        out.append(2)
    if "y" in left:
        out.append(4)
    if "z" in left:
        out.append(2)
    return tuple(out)


def remote(src, dst, ssem, rsem, dev):
    return pltpu.make_async_remote_copy(
        src_ref=src, dst_ref=dst, send_sem=ssem, recv_sem=rsem,
        device_id=dev, device_id_type=pl.DeviceIdType.MESH,
    )


def dot_nn(left, right):
    return jnp.dot(left, right, preferred_element_type=jnp.float32)


def dot_nt(left, right):
    return lax.dot_general(left, right, (((1,), (1,)), ((), ())), preferred_element_type=jnp.float32)


def dot_tn(left, right):
    return lax.dot_general(left, right, (((0,), (0,)), ((), ())), preferred_element_type=jnp.float32)


def head_diagonal(full):
    low = lax.broadcasted_iota(jnp.int32, (64, 128), 1) < 64
    first = jnp.where(low, full[0:64, 0:128], full[64:128, 0:128])
    second = jnp.where(low, full[128:192, 128:256], full[192:256, 128:256])
    return jnp.concatenate([first, second], axis=1)


def pack_columns(slab):
    parts = slab.reshape(7, 4, 8, 128)
    place = lax.broadcasted_iota(jnp.int32, (7, 8, 128), 1)
    one = pltpu.roll(parts[:, 1], 6, 1)
    two = pltpu.roll(parts[:, 2], 4, 1)
    three = pltpu.roll(parts[:, 3], 2, 1)
    return (
        jnp.where(place < 6, parts[:, 0], one),
        jnp.where(place < 4, one, two),
        jnp.where(place < 2, two, three),
    )


def unpack_columns(first, second, third):
    place = lax.broadcasted_iota(jnp.int32, (7, 8, 128), 1)
    rows = (
        first,
        pltpu.roll(jnp.where(place < 4, second, first), 2, 1),
        pltpu.roll(jnp.where(place < 2, third, second), 4, 1),
        pltpu.roll(third, 6, 1),
    )
    return jnp.stack(rows, axis=1).reshape(28, 8, 128)


def sublayer_kernel(
    inv_root,
    weights, tokens, cotangent, tissue, gain,
    block_output, input_grad, weight_grads,
    normed, branch, mask, attended, gproj, weight_vmem, grad_normed,
    pad, queries, upstream, bias, acc,
    side_send, side_recv, back_send, back_recv, rows_send, rows_recv,
    at_own, at_mate, b_mate, last_send, last_recv,
    load_sem, rows_ss, rows_rs, up_ss, up_rs, side_ss, side_rs, back_ss, back_rs,
    far_ss, far_rs, farb_ss, farb_rs,
    swap_ss, swap_rs, grad_ss, grad_rs, ring_ss, ring_rs,
    *ring_bufs,
):
    f32, bf16 = jnp.float32, jnp.bfloat16
    slide = lax.axis_index("slide")
    gy = lax.axis_index("gy")
    gx = lax.axis_index("gx")
    _, y, z, core = coords()
    along = ((slide, gy - 1, gx), (slide, gy + 1, gx))
    has_along = (gy > 0, gy < 7)
    outer = (gx == 0) | (gx == 3)
    inner = jnp.logical_not(outer)
    mate = mate_id()
    high = 1 - z // 2
    far = (slide, gy, jnp.where(outer, 3 * high, high + 1))

    loads = []
    for g in range(4):
        for kv in range(2):
            columns = slice(1024 * (kv + 1) + 256 * g, 1024 * (kv + 1) + 256 * g + 256)
            loads.append(
                pltpu.make_async_copy(
                    weights.at[:, columns], weight_vmem.at[:, columns], load_sem.at[2 * g + kv]
                )
            )
    for n, columns in ((8, slice(0, 1024)), (9, slice(3072, 4096))):
        loads.append(
            pltpu.make_async_copy(weights.at[:, columns], weight_vmem.at[:, columns], load_sem.at[n])
        )
    for load in loads:
        load.start()

    barrier = pltpu.get_barrier_semaphore()
    greeted = [mate, (slide, (gy + 7) % 8, gx), (slide, (gy + 1) % 8, gx), far]
    greeted += [neighbour(axis, by) for axis in "xyz" for by in (1, -1, 2)]
    for dev in greeted:
        pl.semaphore_signal(barrier, inc=1, device_id=dev, device_id_type=pl.DeviceIdType.MESH)
    flags = tissue[...].astype(f32)
    place = lax.broadcasted_iota(jnp.int32, (16, 16, 16), 1) == lax.broadcasted_iota(jnp.int32, (16, 16, 16), 2)
    picked = jnp.where(place, jnp.broadcast_to(flags[:, None, :], (16, 16, 16)), 0.0)
    mask[...] = jnp.sum(picked, axis=2, keepdims=True).reshape(256, 1)

    def norm_forward(n, carry):
        rows = pl.ds(pl.multiple_of(64 * n, 64), 64)
        wide = tokens[rows, :].astype(f32)
        centred = wide - jnp.mean(wide, axis=1, keepdims=True)
        inverse = lax.rsqrt(jnp.mean(centred * centred, axis=1, keepdims=True) + EPSILON)
        normed[rows, :] = (centred * inverse * gain[...]).astype(bf16)
        branch[n] = (mask[rows, :] * cotangent[rows, :].astype(f32)).astype(bf16)
        return carry

    lax.fori_loop(0, 4, norm_forward, 0)
    pl.semaphore_wait(barrier, len(greeted))

    def rows_copy(g, side):
        src = (6, 16)[side]
        dst = (22, 0)[side]
        return remote(
            pad.at[g, :, src : src + 6, 0:16, :], pad.at[g, :, dst : dst + 6, 0:16, :],
            rows_ss.at[g, side], rows_rs.at[g, side], along[side],
        )

    def mate_copy(g, sent, got, ss, rs):
        return remote(sent.at[g, 1 - core], got.at[g, 1 - core], ss.at[g], rs.at[g], mate)

    def far_copy(g, sent, got, ss, rs):
        return remote(sent.at[g, core], got.at[g, core], ss.at[g], rs.at[g], far)

    side_set = (side_send, side_recv)
    back_set = (back_send, back_recv)

    def side_start(g):
        mate_copy(g, *side_set, side_ss, side_rs).start()

        @pl.when(inner)
        def _():
            far_copy(g, *side_set, far_ss, far_rs).start()

    def side_wait(g):
        mate_copy(g, *side_set, side_ss, side_rs).wait_recv()

        @pl.when(inner)
        def _():
            far_copy(g, *side_set, far_ss, far_rs).wait_recv()

    def back_start(g):
        mate_copy(g, *back_set, back_ss, back_rs).start()

        @pl.when(inner)
        def _():
            far_copy(g, *back_set, farb_ss, farb_rs).start()

    def back_wait(g):
        mate_copy(g, *back_set, back_ss, back_rs).wait_recv()

        @pl.when(inner)
        def _():
            far_copy(g, *back_set, farb_ss, farb_rs).wait_recv()

    def drain(g):
        mate_copy(g, *side_set, side_ss, side_rs).wait_send()
        mate_copy(g, *back_set, back_ss, back_rs).wait_send()

        @pl.when(inner)
        def _():
            far_copy(g, *side_set, far_ss, far_rs).wait_send()
            far_copy(g, *back_set, farb_ss, farb_rs).wait_send()

        for side in range(2):
            @pl.when(has_along[side])
            def _(side=side):
                rows_copy(g, side).wait_send()
                up_copy(g, side).wait_send()

    def up_copy(g, side):
        return remote(
            rows_send.at[g, side], rows_recv.at[g, side], up_ss.at[g, side], up_rs.at[g, side], along[side]
        )

    for g in range(4):
        for kv in range(2):
            loads[2 * g + kv].wait()
            columns = slice(1024 * (kv + 1) + 256 * g, 1024 * (kv + 1) + 256 * g + 256)
            made = dot_nn(normed[...], weight_vmem[:, columns]).astype(bf16)
            pad[g, kv, 6:22, 0:16, :] = made.reshape(16, 16, 256)
        for side in range(2):
            @pl.when(has_along[side])
            def _(g=g, side=side):
                rows_copy(g, side).start()

    for b in range(4):
        shape = (512, 128)
        key = lax.broadcasted_iota(jnp.int32, shape, 0)
        lane = lax.broadcasted_iota(jnp.int32, shape, 1) & 63
        key_row, slot = key >> 5, key & 31
        key_col = jnp.where(slot < 24, slot, slot - 30)
        down = key_row - (lane >> 4)
        aside = key_col - (lane & 15)
        grid_row = key_row + (gy * 16 + 4 * b - 6)
        grid_col = key_col + gx * 16
        allowed = (slot < 30) & (down >= 0) & (down <= 12) & (aside >= -6) & (aside <= 6)
        allowed = allowed & (grid_row >= 0) & (grid_row < 128) & (grid_col >= 0) & (grid_col < 64)
        half = jnp.where(allowed, 0.0, -1e30).astype(f32)
        bias[b] = jnp.concatenate([half, half], axis=1)

    def prepare(g):
        for side in range(2):
            zero_row = (22, 0)[side]

            @pl.when(has_along[side])
            def _(g=g, side=side):
                rows_copy(g, 1 - side).wait_recv()

            @pl.when(jnp.logical_not(has_along[side]))
            def _(g=g, zero_row=(0, 22)[side]):
                pad[g, :, zero_row : zero_row + 6, 0:16, :] = jnp.zeros((2, 6, 16, 256), bf16)

        tile_part = pad[g, :, :, 0:16, :].astype(f32)
        for piece in range(4):
            lanes = slice(128 * (piece % 2), 128 * (piece % 2) + 128)
            part = tile_part[piece // 2, :, :, lanes]
            for side, slab in ((0, part[:, 0:8]), (1, pltpu.roll(part[:, 8:16], 6, 1))):
                for n, packed in enumerate(pack_columns(slab)):
                    side_send[g, side, piece, :, n] = packed.astype(bf16)
        side_start(g)

    @pl.when(outer)
    def _():
        side_recv[:, pl.ds(1 - core, 1)] = jnp.zeros((4, 1, 4, 7, 3, 8, 128), bf16)
        back_recv[:, pl.ds(1 - core, 1)] = jnp.zeros((4, 1, 4, 7, 3, 8, 128), bf16)

    same_head = (lax.broadcasted_iota(jnp.int32, (256, 256), 0) >> 6) == (
        lax.broadcasted_iota(jnp.int32, (256, 256), 1) >> 6
    )
    head_mask = jnp.where(same_head, 1.0, 0.0).astype(bf16)

    def attend(g):
        columns = slice(256 * g, 256 * g + 256)
        acc[g] = jnp.zeros((2, 28, 32, 256), f32)

        def block(b, carry):
            keys = pad[g, 0, pl.ds(4 * b, 16)].reshape(512, 256)
            values = pad[g, 1, pl.ds(4 * b, 16)].reshape(512, 256)
            query = queries[b, :, columns]
            grad = upstream[b, :, columns]
            query_heads = jnp.concatenate([query] * 4, axis=0) * head_mask
            grad_heads = jnp.concatenate([grad] * 4, axis=0) * head_mask
            scores = dot_nt(keys, query_heads) + bias[b]
            top = jnp.max(scores, axis=0, keepdims=True)
            exponent = jnp.exp(scores - top)
            total = jnp.sum(exponent, axis=0, keepdims=True)
            probs = exponent * (1.0 / total)
            probs_bf = probs.astype(bf16)
            grad_probs = dot_nt(values, grad_heads)
            centre = jnp.sum(probs * grad_probs, axis=0, keepdims=True)
            grad_scores = (probs * (grad_probs - centre)).astype(bf16)
            attended[b, :, columns] = head_diagonal(dot_tn(probs_bf, values)).astype(bf16)
            gproj[b, :, columns] = (head_diagonal(dot_tn(grad_scores, keys)) * 0.125).astype(bf16)
            rows = pl.ds(4 * b, 16)
            acc[g, 0, rows] += dot_nn(grad_scores, query_heads).reshape(16, 32, 256)
            acc[g, 1, rows] += dot_nn(probs_bf, grad_heads).reshape(16, 32, 256)
            return carry

        lax.fori_loop(0, 4, block, 0)

    def start_back(g):
        for piece in range(4):
            lanes = slice(128 * (piece % 2), 128 * (piece % 2) + 128)
            for side, lo in ((0, 24), (1, 16)):
                for n, packed in enumerate(pack_columns(acc[g, piece // 2, :, lo : lo + 8, lanes])):
                    back_send[g, side, piece, :, n] = packed.astype(bf16)
        back_start(g)

    def start_up(g):
        back_wait(g)
        place = lax.broadcasted_iota(jnp.int32, (28, 8, 128), 1)
        for piece in range(4):
            lanes = slice(128 * (piece % 2), 128 * (piece % 2) + 128)
            low, high = [
                jnp.where(
                    place < 6,
                    unpack_columns(*[back_recv[g, n, piece, :, m].astype(f32) for m in range(3)]),
                    0.0,
                )
                for n in (1, 0)
            ]
            acc[g, piece // 2, :, 0:8, lanes] += low
            acc[g, piece // 2, :, 8:16, lanes] += pltpu.roll(high, 2, 1)
        rows_send[g, 0] = acc[g, :, 0:6, 0:16, :].astype(bf16)
        rows_send[g, 1] = acc[g, :, 22:28, 0:16, :].astype(bf16)
        for side in range(2):
            @pl.when(has_along[side])
            def _(side=side):
                up_copy(g, side).start()

    def finish(g):
        for side in range(2):
            lo = (6, 16)[side]

            @pl.when(has_along[side])
            def _(side=side, lo=lo):
                up_copy(g, 1 - side).wait_recv()
                acc[g, :, lo : lo + 6, 0:16, :] += rows_recv[g, 1 - side].astype(f32)

        for kv in range(2):
            lo = 1024 * (kv + 1) + 256 * g
            gproj[:, :, lo : lo + 256] = acc[g, kv, 6:22, 0:16, :].reshape(4, 64, 256).astype(bf16)
            grad_swap(kv + 1, g)

    def unpack(g):
        side_wait(g)
        for piece in range(4):
            lanes = slice(128 * (piece % 2), 128 * (piece % 2) + 128)
            slabs = [
                unpack_columns(*[side_recv[g, n, piece, :, m].astype(f32) for m in range(3)]) for n in range(2)
            ]
            pad[g, piece // 2, :, 16:32, lanes] = jnp.concatenate(slabs, axis=1).astype(bf16)

    def grad_copy(j, g):
        lo = 1024 * j + 256 * g
        half = g % 2
        return remote(
            gproj.at[:, :, lo : lo + 256], b_mate.at[j, half], grad_ss.at[j, half], grad_rs.at[j, half], mate
        )

    def grad_swap(j, g):
        @pl.when(core != g // 2)
        def _():
            grad_copy(j, g).start()

    def left_copy(kind, n):
        return remote(
            at_own.at[kind, n], at_mate.at[kind, n], swap_ss.at[kind, n], swap_rs.at[kind, n], mate
        )

    branch_copies = []
    for half in range(2):
        lo = pl.multiple_of((1 - core) * 512 + 256 * half, 256)
        branch_copies.append(
            remote(branch.at[:, :, pl.ds(lo, 256)], b_mate.at[3, half], grad_ss.at[3, half], grad_rs.at[3, half], mate)
        )

    sbuf = [[ring_bufs[c * 3 + p] for p in range(3)] for c in range(4)]
    rbuf = [[ring_bufs[12 + c * 3 + p] for p in range(3)] for c in range(4)]
    keep = [[ring_bufs[24 + c * 3 + p] for p in range(3)] for c in range(4)]
    part = [[ring_bufs[36 + c * 3 + p] for p in range(3)] for c in range(4)]

    def ring_copy(c, p, s):
        by = 1 if s in (0, 2, 4) else -1
        if p >= DIRECT_FROM and s < 2:
            by = 2
        return remote(
            sbuf[c][p].at[s], rbuf[c][p].at[s],
            ring_ss.at[c, p, s], ring_rs.at[c, p, s], neighbour(CHUNK_AXES[c][p], by),
        )

    def ring_block(c, p, by):
        axis = CHUNK_AXES[c][p]
        j = (axis_coord(axis) + by + 4) % 4
        if p > 0:
            return part[c][p - 1][pick(None, CHUNK_AXES[c][p:], axis, j)].reshape(256 >> (2 * p), 512)
        kind = 1 if c == 3 else 0
        index = (kind,) + pick(None, "xyz", axis, j)
        left_own = at_own[index].reshape(256, 256)
        left_mate = at_mate[index].reshape(256, 256)
        base = 0 if c == 3 else 1024 * c
        columns = pl.ds(pl.multiple_of(base + 512 * core, 512), 512)
        right_own = (branch if c == 3 else gproj)[:, :, columns].reshape(256, 512)
        right_mate = jnp.concatenate([b_mate[c, 0].reshape(256, 256), b_mate[c, 1].reshape(256, 256)], axis=1)
        return dot_nn(left_own, right_own) + dot_nn(left_mate, right_mate)

    def ring_start(c, p):
        value = ring_block(c, p, 2)
        sbuf[c][p][0] = value[:, :256].astype(bf16)
        ring_copy(c, p, 0).start()
        sbuf[c][p][1] = value[:, 256:].astype(bf16)
        ring_copy(c, p, 1).start()
        value = ring_block(c, p, 1)
        sbuf[c][p][2] = value[:, 256:].astype(bf16)
        ring_copy(c, p, 2).start()
        if p >= DIRECT_FROM:
            sbuf[c][p][4] = value[:, :256].astype(bf16)
            ring_copy(c, p, 4).start()
        else:
            keep[c][p][0] = value[:, :256]
        value = ring_block(c, p, -1)
        sbuf[c][p][3] = value[:, :256].astype(bf16)
        ring_copy(c, p, 3).start()
        if p >= DIRECT_FROM:
            sbuf[c][p][5] = value[:, 256:].astype(bf16)
            ring_copy(c, p, 5).start()
        else:
            keep[c][p][1] = value[:, 256:]
        part[c][p][...] = ring_block(c, p, 0).reshape(part[c][p].shape)

    def ring_relay(c, p):
        if p >= DIRECT_FROM:
            return
        for s in (0, 1):
            ring_copy(c, p, s).wait_recv()
            sbuf[c][p][4 + s] = (keep[c][p][s] + rbuf[c][p][s].astype(f32)).astype(bf16)
            ring_copy(c, p, 4 + s).start()

    def ring_finish(c, p):
        for s in (2, 3, 4, 5):
            ring_copy(c, p, s).wait_recv()
        shape = part[c][p].shape[:-1] + (256,)
        first = rbuf[c][p][3].astype(f32) + rbuf[c][p][4].astype(f32)
        second = rbuf[c][p][2].astype(f32) + rbuf[c][p][5].astype(f32)
        if p >= DIRECT_FROM:
            ring_copy(c, p, 0).wait_recv()
            ring_copy(c, p, 1).wait_recv()
            first = first + rbuf[c][p][0].astype(f32)
            second = second + rbuf[c][p][1].astype(f32)
        part[c][p][..., :256] += first.reshape(shape)
        part[c][p][..., 256:] += second.reshape(shape)

    def swap_wait(c):
        for half in range(2):
            grad_copy(c, half).wait_recv()

    def attend_all(g):
        unpack(g)
        attend(g)
        start_back(g)
        grad_swap(0, g)
        columns = slice(256 * g, 256 * g + 256)
        at_own[1, g] = attended[:, :, columns].reshape(256, 256).T.reshape(2, 4, 2, 16, 256)
        left_copy(1, g).start()

    for n in range(4):
        columns = slice(256 * n, 256 * n + 256)
        at_own[0, n] = normed[:, columns].T.reshape(2, 4, 2, 16, 256)
        left_copy(0, n).start()
    for copy in branch_copies:
        copy.start()
    loads[8].wait()
    for n in range(4):
        columns = slice(256 * n, 256 * n + 256)
        made = dot_nn(normed[...], weight_vmem[:, columns]).astype(bf16) * jnp.asarray(0.125, bf16)
        queries[:, :, columns] = made.reshape(4, 64, 256)
    loads[9].wait()
    flat = branch[...].reshape(256, 1024)
    for n in range(4):
        columns = slice(256 * n, 256 * n + 256)
        made = dot_nt(flat, weight_vmem[columns, 3072:4096]).astype(bf16)
        upstream[:, :, columns] = made.reshape(4, 64, 256)
    prepare(0)
    prepare(1)
    attend_all(0)
    prepare(2)
    attend_all(1)
    prepare(3)
    start_up(0)
    attend_all(2)
    start_up(1)
    finish(0)
    attend_all(3)
    start_up(2)
    finish(1)
    for n in range(4):
        left_copy(0, n).wait_recv()
        left_copy(1, n).wait_recv()
    for copy in branch_copies:
        copy.wait_recv()
    swap_wait(0)
    ring_start(0, 0)
    start_up(3)
    finish(2)
    ring_start(3, 0)
    ring_relay(0, 0)
    finish(3)
    for c in (1, 2):
        swap_wait(c)
        ring_start(c, 0)
    ring_relay(3, 0)
    flat = attended[...].reshape(256, 1024)
    for n in range(4):
        columns = slice(256 * n, 256 * n + 256)
        product = dot_nn(flat, weight_vmem[:, 3072 + 256 * n : 3328 + 256 * n])
        block_output[:, columns] = (tokens[:, columns].astype(f32) + mask[...] * product).astype(bf16)
    ring_relay(1, 0)
    ring_relay(2, 0)
    flat = gproj[...].reshape(256, 3072)
    for n in range(4):
        rows = slice(256 * n, 256 * n + 256)
        grad_normed[:, rows] = dot_nt(flat, weight_vmem[rows, 0:3072])
    for c in (0, 3, 1, 2):
        ring_finish(c, 0)
        ring_start(c, 1)
    for c in (0, 3, 1, 2):
        ring_relay(c, 1)

    def norm_rows(n, carry):
        rows = pl.ds(pl.multiple_of(64 * n, 64), 64)
        wide = tokens[rows, :].astype(f32)
        centred = wide - jnp.mean(wide, axis=1, keepdims=True)
        inverse = lax.rsqrt(jnp.mean(centred * centred, axis=1, keepdims=True) + EPSILON)
        normalized = centred * inverse
        scaled = grad_normed[rows, :] * gain[...]
        first_mean = jnp.mean(scaled, axis=1, keepdims=True)
        second_mean = jnp.mean(scaled * normalized, axis=1, keepdims=True)
        grad = cotangent[rows, :].astype(f32) + inverse * (scaled - first_mean - normalized * second_mean)
        input_grad[rows, :] = grad.astype(bf16)
        return carry

    lax.fori_loop(0, 4, norm_rows, 0)
    for c in (0, 3, 1, 2):
        ring_finish(c, 1)
        ring_start(c, 2)
    for c in (0, 3, 1, 2):
        ring_relay(c, 2)
    for c in (0, 3, 1, 2):
        ring_finish(c, 2)
        value = part[c][2][...] * inv_root
        mine = jnp.where(core == 0, value[:8], value[8:])
        theirs = jnp.where(core == 0, value[8:], value[:8])
        last_send[c] = theirs
        final_copy = remote(last_send.at[c], last_recv.at[c], swap_ss.at[2, c], swap_rs.at[2, c], mate)
        final_copy.start()
        offset = pl.multiple_of(1024 * c + 512 * core, 512)
        weight_grads[:, pl.ds(offset, 512)] = mine
    for c in (0, 3, 1, 2):
        final_copy = remote(last_send.at[c], last_recv.at[c], swap_ss.at[2, c], swap_rs.at[2, c], mate)
        final_copy.wait_recv()
        offset = pl.multiple_of(1024 * c + 512 * (1 - core), 512)
        weight_grads[:, pl.ds(offset, 512)] = last_recv[c]
        final_copy.wait_send()
        for p in range(3):
            for s in range(6):
                ring_copy(c, p, s).wait_send()
    for n in range(4):
        left_copy(0, n).wait_send()
        left_copy(1, n).wait_send()
        drain(n)
        for j in range(3):
            @pl.when(core != n // 2)
            def _(j=j, n=n):
                grad_copy(j, n).wait_send()
    for copy in branch_copies:
        copy.wait_send()


def sublayer(weights, tokens, cotangent, tissue, gain, inv_root):
    bf16, f32 = jnp.bfloat16, jnp.float32
    dma = pltpu.SemaphoreType.DMA
    any_space = pl.BlockSpec(memory_space=pl.ANY)
    vmem = pl.BlockSpec(memory_space=pltpu.VMEM)
    ring = []
    for _ in range(2):
        for c in range(4):
            for p in range(3):
                ring.append(pltpu.VMEM((6, 256 >> (2 * p), 256), bf16))
    for c in range(4):
        for p in range(3):
            ring.append(pltpu.VMEM((2, 256 >> (2 * p), 256), f32))
    for c in range(4):
        for p in range(3):
            ring.append(pltpu.VMEM(row_dims(CHUNK_AXES[c][p + 1 :]) + (16, 512), f32))
    slab = pltpu.VMEM((4, 2, 4, 7, 3, 8, 128), bf16)
    return pl.pallas_call(
        functools.partial(sublayer_kernel, inv_root),
        out_shape=(
            jax.ShapeDtypeStruct((256, 1024), bf16),
            jax.ShapeDtypeStruct((256, 1024), bf16),
            jax.ShapeDtypeStruct((8, 4096), f32),
        ),
        in_specs=[any_space] + [vmem] * 4,
        out_specs=(vmem,) * 3,
        scratch_shapes=[
            pltpu.VMEM((256, 1024), bf16),
            pltpu.VMEM((4, 64, 1024), bf16),
            pltpu.VMEM((256, 1), f32),
            pltpu.VMEM((4, 64, 1024), bf16),
            pltpu.VMEM((4, 64, 3072), bf16),
            pltpu.VMEM((1024, 4096), bf16),
            pltpu.VMEM((256, 1024), f32),
            pltpu.VMEM((4, 2, 28, 32, 256), bf16),
            pltpu.VMEM((4, 64, 1024), bf16),
            pltpu.VMEM((4, 64, 1024), bf16),
            pltpu.VMEM((4, 512, 256), f32),
            pltpu.VMEM((4, 2, 28, 32, 256), f32),
            slab, slab, slab, slab,
            pltpu.VMEM((4, 2, 2, 6, 16, 256), bf16),
            pltpu.VMEM((4, 2, 2, 6, 16, 256), bf16),
            pltpu.VMEM((2, 4, 2, 4, 2, 16, 256), bf16),
            pltpu.VMEM((2, 4, 2, 4, 2, 16, 256), bf16),
            pltpu.VMEM((4, 2, 4, 64, 256), bf16),
            pltpu.VMEM((4, 8, 512), f32),
            pltpu.VMEM((4, 8, 512), f32),
            dma((10,)),
        ]
        + [dma((4, 2))] * 4
        + [dma((4,))] * 8
        + [dma((3, 4))] * 2
        + [dma((4, 2))] * 2
        + [dma((4, 3, 6))] * 2
        + ring,
        compiler_params=pltpu.CompilerParams(
            collective_id=0, has_side_effects=True, vmem_limit_bytes=67043328
        ),
    )(weights, tokens, cotangent, tissue, gain)


def place_kernel(*refs):
    for source, target in zip(refs[:3], refs[3:]):
        target[...] = source[...]


def place(*arrays):
    vmem = pl.BlockSpec(memory_space=pltpu.VMEM)
    return pl.pallas_call(
        place_kernel,
        out_shape=tuple(jax.ShapeDtypeStruct(a.shape, a.dtype) for a in arrays),
        in_specs=[vmem] * 3,
        out_specs=(vmem,) * 3,
    )(*arrays)


def local(tokens, weights, norm_gain, tissue, cotangent):
    model_width = tokens.shape[-1]
    token_count = tokens.shape[1] * tokens.shape[2]
    group_count = lax.axis_size("slide") * lax.axis_size("gy") * lax.axis_size("gx")
    inv_root = 1.0 / math.sqrt(group_count * token_count)
    block_output, input_grad, weight_grads = sublayer(
        weights,
        tokens.reshape(token_count, model_width),
        cotangent.reshape(token_count, model_width),
        tissue[0],
        norm_gain.reshape(1, model_width),
        inv_root,
    )
    block_output, input_grad, weight_grads = place(block_output, input_grad, weight_grads)
    return (block_output.reshape(tokens.shape), input_grad.reshape(tokens.shape), weight_grads)


def solution(mesh):
    in_specs = (
        P("slide", "gy", "gx", None),
        P(),
        P(),
        P("slide", "gy", "gx"),
        P("slide", "gy", "gx", None),
    )
    out_specs = (
        P("slide", "gy", "gx", None),
        P("slide", "gy", "gx", None),
        P(("slide", "gy", "gx"), None),
    )
    return jax.shard_map(local, mesh=mesh, in_specs=in_specs, out_specs=out_specs, check_vma=False)
```

```python
import functools
import math

import jax
import jax.numpy as jnp
from jax import lax
from jax.experimental import pallas as pl
from jax.experimental.pallas import tpu as pltpu
from jax.sharding import PartitionSpec as P

EPSILON = 1e-06


DIRECT_FROM = 1
CHUNK_AXES = ("xyz", "yzx", "xzy", "zyx")


def coords():
    x = lax.axis_index("slide")
    gy = lax.axis_index("gy")
    gx = lax.axis_index("gx")
    zlo, y = gy // 4, gy % 4
    zhi, core = gx // 2, gx % 2
    return x, y, zhi * 2 + zlo, core


def device_at(x, y, z, core):
    return (x, (z % 2) * 4 + y, (z // 2) * 2 + core)


def neighbour(axis, by):
    x, y, z, core = coords()
    if axis == "x":
        return device_at((x + by + 4) % 4, y, z, core)
    if axis == "y":
        return device_at(x, (y + by + 4) % 4, z, core)
    return device_at(x, y, (z + by + 4) % 4, core)


def mate_id():
    x, y, z, core = coords()
    return device_at(x, y, z, 1 - core)


def axis_coord(axis):
    x, y, z, _ = coords()
    return {"x": x, "y": y, "z": z}[axis]


def pick(ref, left, axis, j):
    dims = [d for d in ("x", "l", "y", "h") if (d in left) or (d in "lh" and "z" in left)]
    index = []
    for d in dims:
        if d == axis:
            index.append(j)
        elif axis == "z" and d == "l":
            index.append(j % 2)
        elif axis == "z" and d == "h":
            index.append(j // 2)
        else:
            index.append(slice(None))
    return tuple(index)


def row_dims(left):
    out = []
    if "x" in left:
        out.append(4)
    if "z" in left:
        out.append(2)
    if "y" in left:
        out.append(4)
    if "z" in left:
        out.append(2)
    return tuple(out)


def remote(src, dst, ssem, rsem, dev):
    return pltpu.make_async_remote_copy(
        src_ref=src, dst_ref=dst, send_sem=ssem, recv_sem=rsem,
        device_id=dev, device_id_type=pl.DeviceIdType.MESH,
    )


def dot_nn(left, right):
    return jnp.dot(left, right, preferred_element_type=jnp.float32)


def dot_nt(left, right):
    return lax.dot_general(left, right, (((1,), (1,)), ((), ())), preferred_element_type=jnp.float32)


def dot_tn(left, right):
    return lax.dot_general(left, right, (((0,), (0,)), ((), ())), preferred_element_type=jnp.float32)


def head_diagonal(full):
    low = lax.broadcasted_iota(jnp.int32, (64, 128), 1) < 64
    first = jnp.where(low, full[0:64, 0:128], full[64:128, 0:128])
    second = jnp.where(low, full[128:192, 128:256], full[192:256, 128:256])
    return jnp.concatenate([first, second], axis=1)


def pack_columns(slab):
    parts = slab.reshape(7, 4, 8, 128)
    place = lax.broadcasted_iota(jnp.int32, (7, 8, 128), 1)
    one = pltpu.roll(parts[:, 1], 6, 1)
    two = pltpu.roll(parts[:, 2], 4, 1)
    three = pltpu.roll(parts[:, 3], 2, 1)
    return (
        jnp.where(place < 6, parts[:, 0], one),
        jnp.where(place < 4, one, two),
        jnp.where(place < 2, two, three),
    )


def unpack_columns(first, second, third):
    place = lax.broadcasted_iota(jnp.int32, (7, 8, 128), 1)
    rows = (
        first,
        pltpu.roll(jnp.where(place < 4, second, first), 2, 1),
        pltpu.roll(jnp.where(place < 2, third, second), 4, 1),
        pltpu.roll(third, 6, 1),
    )
    return jnp.stack(rows, axis=1).reshape(28, 8, 128)


def sublayer_kernel(
    inv_root,
    weights, tokens, cotangent, tissue, gain,
    block_output, input_grad, weight_grads,
    normed, branch, mask, attended, gproj, weight_vmem, grad_normed,
    pad, queries, upstream, bias, acc,
    side_send, side_recv, back_send, back_recv, rows_send, rows_recv,
    at_own, at_mate, b_mate, last_send, last_recv,
    load_sem, rows_ss, rows_rs, up_ss, up_rs, side_ss, side_rs, back_ss, back_rs,
    far_ss, far_rs, farb_ss, farb_rs,
    swap_ss, swap_rs, grad_ss, grad_rs, ring_ss, ring_rs,
    *ring_bufs,
):
    f32, bf16 = jnp.float32, jnp.bfloat16
    slide = lax.axis_index("slide")
    gy = lax.axis_index("gy")
    gx = lax.axis_index("gx")
    _, y, z, core = coords()
    along = ((slide, gy - 1, gx), (slide, gy + 1, gx))
    has_along = (gy > 0, gy < 7)
    outer = (gx == 0) | (gx == 3)
    inner = jnp.logical_not(outer)
    mate = mate_id()
    high = 1 - z // 2
    far = (slide, gy, jnp.where(outer, 3 * high, high + 1))

    loads = []
    for g in range(4):
        for kv in range(2):
            columns = slice(1024 * (kv + 1) + 256 * g, 1024 * (kv + 1) + 256 * g + 256)
            loads.append(
                pltpu.make_async_copy(
                    weights.at[:, columns], weight_vmem.at[:, columns], load_sem.at[2 * g + kv]
                )
            )
    for n, columns in ((8, slice(0, 1024)), (9, slice(3072, 4096))):
        loads.append(
            pltpu.make_async_copy(weights.at[:, columns], weight_vmem.at[:, columns], load_sem.at[n])
        )
    for load in loads:
        load.start()

    barrier = pltpu.get_barrier_semaphore()
    greeted = [mate, (slide, (gy + 7) % 8, gx), (slide, (gy + 1) % 8, gx), far]
    greeted += [neighbour(axis, by) for axis in "xyz" for by in (1, -1, 2)]
    for dev in greeted:
        pl.semaphore_signal(barrier, inc=1, device_id=dev, device_id_type=pl.DeviceIdType.MESH)
    flags = tissue[...].astype(f32)
    place = lax.broadcasted_iota(jnp.int32, (16, 16, 16), 1) == lax.broadcasted_iota(jnp.int32, (16, 16, 16), 2)
    picked = jnp.where(place, jnp.broadcast_to(flags[:, None, :], (16, 16, 16)), 0.0)
    mask[...] = jnp.sum(picked, axis=2, keepdims=True).reshape(256, 1)

    def norm_forward(n, carry):
        rows = pl.ds(pl.multiple_of(64 * n, 64), 64)
        wide = tokens[rows, :].astype(f32)
        centred = wide - jnp.mean(wide, axis=1, keepdims=True)
        inverse = lax.rsqrt(jnp.mean(centred * centred, axis=1, keepdims=True) + EPSILON)
        normed[rows, :] = (centred * inverse * gain[...]).astype(bf16)
        branch[n] = (mask[rows, :] * cotangent[rows, :].astype(f32)).astype(bf16)
        return carry

    lax.fori_loop(0, 4, norm_forward, 0)
    pl.semaphore_wait(barrier, len(greeted))

    def rows_copy(g, side):
        src = (6, 16)[side]
        dst = (22, 0)[side]
        return remote(
            pad.at[g, :, src : src + 6, 0:16, :], pad.at[g, :, dst : dst + 6, 0:16, :],
            rows_ss.at[g, side], rows_rs.at[g, side], along[side],
        )

    def mate_copy(g, sent, got, ss, rs):
        return remote(sent.at[g, 1 - core], got.at[g, 1 - core], ss.at[g], rs.at[g], mate)

    def far_copy(g, sent, got, ss, rs):
        return remote(sent.at[g, core], got.at[g, core], ss.at[g], rs.at[g], far)

    side_set = (side_send, side_recv)
    back_set = (back_send, back_recv)

    def side_start(g):
        mate_copy(g, *side_set, side_ss, side_rs).start()

        @pl.when(inner)
        def _():
            far_copy(g, *side_set, far_ss, far_rs).start()

    def side_wait(g):
        mate_copy(g, *side_set, side_ss, side_rs).wait_recv()

        @pl.when(inner)
        def _():
            far_copy(g, *side_set, far_ss, far_rs).wait_recv()

    def back_start(g):
        mate_copy(g, *back_set, back_ss, back_rs).start()

        @pl.when(inner)
        def _():
            far_copy(g, *back_set, farb_ss, farb_rs).start()

    def back_wait(g):
        mate_copy(g, *back_set, back_ss, back_rs).wait_recv()

        @pl.when(inner)
        def _():
            far_copy(g, *back_set, farb_ss, farb_rs).wait_recv()

    def drain(g):
        mate_copy(g, *side_set, side_ss, side_rs).wait_send()
        mate_copy(g, *back_set, back_ss, back_rs).wait_send()

        @pl.when(inner)
        def _():
            far_copy(g, *side_set, far_ss, far_rs).wait_send()
            far_copy(g, *back_set, farb_ss, farb_rs).wait_send()

        for side in range(2):
            @pl.when(has_along[side])
            def _(side=side):
                rows_copy(g, side).wait_send()
                up_copy(g, side).wait_send()

    def up_copy(g, side):
        return remote(
            rows_send.at[g, side], rows_recv.at[g, side], up_ss.at[g, side], up_rs.at[g, side], along[side]
        )

    for g in range(4):
        for kv in range(2):
            loads[2 * g + kv].wait()
            columns = slice(1024 * (kv + 1) + 256 * g, 1024 * (kv + 1) + 256 * g + 256)
            made = dot_nn(normed[...], weight_vmem[:, columns]).astype(bf16)
            pad[g, kv, 6:22, 0:16, :] = made.reshape(16, 16, 256)
        for side in range(2):
            @pl.when(has_along[side])
            def _(g=g, side=side):
                rows_copy(g, side).start()

    for b in range(4):
        shape = (512, 128)
        key = lax.broadcasted_iota(jnp.int32, shape, 0)
        lane = lax.broadcasted_iota(jnp.int32, shape, 1) & 63
        key_row, slot = key >> 5, key & 31
        key_col = jnp.where(slot < 24, slot, slot - 30)
        down = key_row - (lane >> 4)
        aside = key_col - (lane & 15)
        grid_row = key_row + (gy * 16 + 4 * b - 6)
        grid_col = key_col + gx * 16
        allowed = (slot < 30) & (down >= 0) & (down <= 12) & (aside >= -6) & (aside <= 6)
        allowed = allowed & (grid_row >= 0) & (grid_row < 128) & (grid_col >= 0) & (grid_col < 64)
        half = jnp.where(allowed, 0.0, -1e30).astype(f32)
        bias[b] = jnp.concatenate([half, half], axis=1)

    def prepare(g):
        for side in range(2):
            zero_row = (22, 0)[side]

            @pl.when(has_along[side])
            def _(g=g, side=side):
                rows_copy(g, 1 - side).wait_recv()

            @pl.when(jnp.logical_not(has_along[side]))
            def _(g=g, zero_row=(0, 22)[side]):
                pad[g, :, zero_row : zero_row + 6, 0:16, :] = jnp.zeros((2, 6, 16, 256), bf16)

        tile_part = pad[g, :, :, 0:16, :].astype(f32)
        for piece in range(4):
            lanes = slice(128 * (piece % 2), 128 * (piece % 2) + 128)
            part = tile_part[piece // 2, :, :, lanes]
            for side, slab in ((0, part[:, 0:8]), (1, pltpu.roll(part[:, 8:16], 6, 1))):
                for n, packed in enumerate(pack_columns(slab)):
                    side_send[g, side, piece, :, n] = packed.astype(bf16)
        side_start(g)

    @pl.when(outer)
    def _():
        side_recv[:, pl.ds(1 - core, 1)] = jnp.zeros((4, 1, 4, 7, 3, 8, 128), bf16)
        back_recv[:, pl.ds(1 - core, 1)] = jnp.zeros((4, 1, 4, 7, 3, 8, 128), bf16)

    same_head = (lax.broadcasted_iota(jnp.int32, (256, 256), 0) >> 6) == (
        lax.broadcasted_iota(jnp.int32, (256, 256), 1) >> 6
    )
    head_mask = jnp.where(same_head, 1.0, 0.0).astype(bf16)

    def attend(g):
        columns = slice(256 * g, 256 * g + 256)
        acc[g] = jnp.zeros((2, 28, 32, 256), f32)

        def block(b, carry):
            keys = pad[g, 0, pl.ds(4 * b, 16)].reshape(512, 256)
            values = pad[g, 1, pl.ds(4 * b, 16)].reshape(512, 256)
            query = queries[b, :, columns]
            grad = upstream[b, :, columns]
            query_heads = jnp.concatenate([query] * 4, axis=0) * head_mask
            grad_heads = jnp.concatenate([grad] * 4, axis=0) * head_mask
            scores = dot_nt(keys, query_heads) + bias[b]
            top = jnp.max(scores, axis=0, keepdims=True)
            exponent = jnp.exp(scores - top)
            total = jnp.sum(exponent, axis=0, keepdims=True)
            probs = exponent * (1.0 / total)
            probs_bf = probs.astype(bf16)
            grad_probs = dot_nt(values, grad_heads)
            centre = jnp.sum(probs * grad_probs, axis=0, keepdims=True)
            grad_scores = (probs * (grad_probs - centre)).astype(bf16)
            attended[b, :, columns] = head_diagonal(dot_tn(probs_bf, values)).astype(bf16)
            gproj[b, :, columns] = (head_diagonal(dot_tn(grad_scores, keys)) * 0.125).astype(bf16)
            rows = pl.ds(4 * b, 16)
            acc[g, 0, rows] += dot_nn(grad_scores, query_heads).reshape(16, 32, 256)
            acc[g, 1, rows] += dot_nn(probs_bf, grad_heads).reshape(16, 32, 256)
            return carry

        lax.fori_loop(0, 4, block, 0)

    def start_back(g):
        for piece in range(4):
            lanes = slice(128 * (piece % 2), 128 * (piece % 2) + 128)
            for side, lo in ((0, 24), (1, 16)):
                for n, packed in enumerate(pack_columns(acc[g, piece // 2, :, lo : lo + 8, lanes])):
                    back_send[g, side, piece, :, n] = packed.astype(bf16)
        back_start(g)

    def start_up(g):
        back_wait(g)
        place = lax.broadcasted_iota(jnp.int32, (28, 8, 128), 1)
        for piece in range(4):
            lanes = slice(128 * (piece % 2), 128 * (piece % 2) + 128)
            low, high = [
                jnp.where(
                    place < 6,
                    unpack_columns(*[back_recv[g, n, piece, :, m].astype(f32) for m in range(3)]),
                    0.0,
                )
                for n in (1, 0)
            ]
            acc[g, piece // 2, :, 0:8, lanes] += low
            acc[g, piece // 2, :, 8:16, lanes] += pltpu.roll(high, 2, 1)
        rows_send[g, 0] = acc[g, :, 0:6, 0:16, :].astype(bf16)
        rows_send[g, 1] = acc[g, :, 22:28, 0:16, :].astype(bf16)
        for side in range(2):
            @pl.when(has_along[side])
            def _(side=side):
                up_copy(g, side).start()

    def finish(g):
        for side in range(2):
            lo = (6, 16)[side]

            @pl.when(has_along[side])
            def _(side=side, lo=lo):
                up_copy(g, 1 - side).wait_recv()
                acc[g, :, lo : lo + 6, 0:16, :] += rows_recv[g, 1 - side].astype(f32)

        for kv in range(2):
            lo = 1024 * (kv + 1) + 256 * g
            gproj[:, :, lo : lo + 256] = acc[g, kv, 6:22, 0:16, :].reshape(4, 64, 256).astype(bf16)
            grad_swap(kv + 1, g)

    def unpack(g):
        side_wait(g)
        for piece in range(4):
            lanes = slice(128 * (piece % 2), 128 * (piece % 2) + 128)
            slabs = [
                unpack_columns(*[side_recv[g, n, piece, :, m].astype(f32) for m in range(3)]) for n in range(2)
            ]
            pad[g, piece // 2, :, 16:32, lanes] = jnp.concatenate(slabs, axis=1).astype(bf16)

    def grad_copy(j, g):
        lo = 1024 * j + 256 * g
        half = g % 2
        return remote(
            gproj.at[:, :, lo : lo + 256], b_mate.at[j, half], grad_ss.at[j, half], grad_rs.at[j, half], mate
        )

    def grad_swap(j, g):
        @pl.when(core != g // 2)
        def _():
            grad_copy(j, g).start()

    def left_copy(kind, n):
        return remote(
            at_own.at[kind, n], at_mate.at[kind, n], swap_ss.at[kind, n], swap_rs.at[kind, n], mate
        )

    branch_copies = []
    for half in range(2):
        lo = pl.multiple_of((1 - core) * 512 + 256 * half, 256)
        branch_copies.append(
            remote(branch.at[:, :, pl.ds(lo, 256)], b_mate.at[3, half], grad_ss.at[3, half], grad_rs.at[3, half], mate)
        )

    sbuf = [[ring_bufs[c * 3 + p] for p in range(3)] for c in range(4)]
    rbuf = [[ring_bufs[12 + c * 3 + p] for p in range(3)] for c in range(4)]
    keep = [[ring_bufs[24 + c * 3 + p] for p in range(3)] for c in range(4)]
    part = [[ring_bufs[36 + c * 3 + p] for p in range(3)] for c in range(4)]

    def ring_copy(c, p, s):
        by = 1 if s in (0, 2, 4) else -1
        if p >= DIRECT_FROM and s < 2:
            by = 2
        return remote(
            sbuf[c][p].at[s], rbuf[c][p].at[s],
            ring_ss.at[c, p, s], ring_rs.at[c, p, s], neighbour(CHUNK_AXES[c][p], by),
        )

    def ring_block(c, p, by):
        axis = CHUNK_AXES[c][p]
        j = (axis_coord(axis) + by + 4) % 4
        if p > 0:
            return part[c][p - 1][pick(None, CHUNK_AXES[c][p:], axis, j)].reshape(256 >> (2 * p), 512)
        kind = 1 if c == 3 else 0
        index = (kind,) + pick(None, "xyz", axis, j)
        left_own = at_own[index].reshape(256, 256)
        left_mate = at_mate[index].reshape(256, 256)
        base = 0 if c == 3 else 1024 * c
        columns = pl.ds(pl.multiple_of(base + 512 * core, 512), 512)
        right_own = (branch if c == 3 else gproj)[:, :, columns].reshape(256, 512)
        right_mate = jnp.concatenate([b_mate[c, 0].reshape(256, 256), b_mate[c, 1].reshape(256, 256)], axis=1)
        return dot_nn(left_own, right_own) + dot_nn(left_mate, right_mate)

    def ring_start(c, p):
        value = ring_block(c, p, 2)
        sbuf[c][p][0] = value[:, :256].astype(bf16)
        ring_copy(c, p, 0).start()
        sbuf[c][p][1] = value[:, 256:].astype(bf16)
        ring_copy(c, p, 1).start()
        value = ring_block(c, p, 1)
        sbuf[c][p][2] = value[:, 256:].astype(bf16)
        ring_copy(c, p, 2).start()
        if p >= DIRECT_FROM:
            sbuf[c][p][4] = value[:, :256].astype(bf16)
            ring_copy(c, p, 4).start()
        else:
            keep[c][p][0] = value[:, :256]
        value = ring_block(c, p, -1)
        sbuf[c][p][3] = value[:, :256].astype(bf16)
        ring_copy(c, p, 3).start()
        if p >= DIRECT_FROM:
            sbuf[c][p][5] = value[:, 256:].astype(bf16)
            ring_copy(c, p, 5).start()
        else:
            keep[c][p][1] = value[:, 256:]
        part[c][p][...] = ring_block(c, p, 0).reshape(part[c][p].shape)

    def ring_relay(c, p):
        if p >= DIRECT_FROM:
            return
        for s in (0, 1):
            ring_copy(c, p, s).wait_recv()
            sbuf[c][p][4 + s] = (keep[c][p][s] + rbuf[c][p][s].astype(f32)).astype(bf16)
            ring_copy(c, p, 4 + s).start()

    def ring_finish(c, p):
        for s in (2, 3, 4, 5):
            ring_copy(c, p, s).wait_recv()
        shape = part[c][p].shape[:-1] + (256,)
        first = rbuf[c][p][3].astype(f32) + rbuf[c][p][4].astype(f32)
        second = rbuf[c][p][2].astype(f32) + rbuf[c][p][5].astype(f32)
        if p >= DIRECT_FROM:
            ring_copy(c, p, 0).wait_recv()
            ring_copy(c, p, 1).wait_recv()
            first = first + rbuf[c][p][0].astype(f32)
            second = second + rbuf[c][p][1].astype(f32)
        part[c][p][..., :256] += first.reshape(shape)
        part[c][p][..., 256:] += second.reshape(shape)

    def swap_wait(c):
        for half in range(2):
            grad_copy(c, half).wait_recv()

    def attend_all(g):
        unpack(g)
        attend(g)
        start_back(g)
        grad_swap(0, g)
        columns = slice(256 * g, 256 * g + 256)
        at_own[1, g] = attended[:, :, columns].reshape(256, 256).T.reshape(2, 4, 2, 16, 256)
        left_copy(1, g).start()

    for n in range(4):
        columns = slice(256 * n, 256 * n + 256)
        at_own[0, n] = normed[:, columns].T.reshape(2, 4, 2, 16, 256)
        left_copy(0, n).start()
    for copy in branch_copies:
        copy.start()
    loads[8].wait()
    for n in range(4):
        columns = slice(256 * n, 256 * n + 256)
        made = dot_nn(normed[...], weight_vmem[:, columns]).astype(bf16) * jnp.asarray(0.125, bf16)
        queries[:, :, columns] = made.reshape(4, 64, 256)
    loads[9].wait()
    flat = branch[...].reshape(256, 1024)
    for n in range(4):
        columns = slice(256 * n, 256 * n + 256)
        made = dot_nt(flat, weight_vmem[columns, 3072:4096]).astype(bf16)
        upstream[:, :, columns] = made.reshape(4, 64, 256)
    prepare(0)
    prepare(1)
    attend_all(0)
    prepare(2)
    attend_all(1)
    prepare(3)
    start_up(0)
    attend_all(2)
    start_up(1)
    finish(0)
    attend_all(3)
    start_up(2)
    finish(1)
    for n in range(4):
        left_copy(0, n).wait_recv()
        left_copy(1, n).wait_recv()
    for copy in branch_copies:
        copy.wait_recv()
    swap_wait(0)
    ring_start(0, 0)
    start_up(3)
    finish(2)
    @pl.when(core == 0)
    def _():
        swap_wait(1)
        ring_start(1, 0)

    @pl.when(core == 1)
    def _():
        ring_start(3, 0)

    ring_relay(0, 0)
    flat = attended[...].reshape(256, 1024)
    for n in range(4):
        columns = slice(256 * n, 256 * n + 256)
        product = dot_nn(flat, weight_vmem[:, 3072 + 256 * n : 3328 + 256 * n])
        block_output[:, columns] = (tokens[:, columns].astype(f32) + mask[...] * product).astype(bf16)
    finish(3)

    @pl.when(core == 0)
    def _():
        swap_wait(2)
        ring_start(2, 0)
        ring_relay(1, 0)
        ring_start(3, 0)
        ring_relay(2, 0)
        ring_relay(3, 0)

    @pl.when(core == 1)
    def _():
        swap_wait(1)
        ring_start(1, 0)
        ring_relay(3, 0)
        swap_wait(2)
        ring_start(2, 0)
        ring_relay(1, 0)
        ring_relay(2, 0)

    flat = gproj[...].reshape(256, 3072)
    for n in range(4):
        rows = slice(256 * n, 256 * n + 256)
        grad_normed[:, rows] = dot_nt(flat, weight_vmem[rows, 0:3072])
    for c in (0, 3, 1, 2):
        ring_finish(c, 0)
        ring_start(c, 1)
    for c in (0, 3, 1, 2):
        ring_relay(c, 1)

    def norm_rows(n, carry):
        rows = pl.ds(pl.multiple_of(64 * n, 64), 64)
        wide = tokens[rows, :].astype(f32)
        centred = wide - jnp.mean(wide, axis=1, keepdims=True)
        inverse = lax.rsqrt(jnp.mean(centred * centred, axis=1, keepdims=True) + EPSILON)
        normalized = centred * inverse
        scaled = grad_normed[rows, :] * gain[...]
        first_mean = jnp.mean(scaled, axis=1, keepdims=True)
        second_mean = jnp.mean(scaled * normalized, axis=1, keepdims=True)
        grad = cotangent[rows, :].astype(f32) + inverse * (scaled - first_mean - normalized * second_mean)
        input_grad[rows, :] = grad.astype(bf16)
        return carry

    lax.fori_loop(0, 4, norm_rows, 0)
    for c in (0, 3, 1, 2):
        ring_finish(c, 1)
        ring_start(c, 2)
    for c in (0, 3, 1, 2):
        ring_relay(c, 2)
    for c in (0, 3, 1, 2):
        ring_finish(c, 2)
        value = part[c][2][...] * inv_root
        mine = jnp.where(core == 0, value[:8], value[8:])
        theirs = jnp.where(core == 0, value[8:], value[:8])
        last_send[c] = theirs
        final_copy = remote(last_send.at[c], last_recv.at[c], swap_ss.at[2, c], swap_rs.at[2, c], mate)
        final_copy.start()
        offset = pl.multiple_of(1024 * c + 512 * core, 512)
        weight_grads[:, pl.ds(offset, 512)] = mine
    for c in (0, 3, 1, 2):
        final_copy = remote(last_send.at[c], last_recv.at[c], swap_ss.at[2, c], swap_rs.at[2, c], mate)
        final_copy.wait_recv()
        offset = pl.multiple_of(1024 * c + 512 * (1 - core), 512)
        weight_grads[:, pl.ds(offset, 512)] = last_recv[c]
        final_copy.wait_send()
        for p in range(3):
            for s in range(6):
                ring_copy(c, p, s).wait_send()
    for n in range(4):
        left_copy(0, n).wait_send()
        left_copy(1, n).wait_send()
        drain(n)
        for j in range(3):
            @pl.when(core != n // 2)
            def _(j=j, n=n):
                grad_copy(j, n).wait_send()
    for copy in branch_copies:
        copy.wait_send()


def sublayer(weights, tokens, cotangent, tissue, gain, inv_root):
    bf16, f32 = jnp.bfloat16, jnp.float32
    dma = pltpu.SemaphoreType.DMA
    any_space = pl.BlockSpec(memory_space=pl.ANY)
    vmem = pl.BlockSpec(memory_space=pltpu.VMEM)
    ring = []
    for _ in range(2):
        for c in range(4):
            for p in range(3):
                ring.append(pltpu.VMEM((6, 256 >> (2 * p), 256), bf16))
    for c in range(4):
        for p in range(3):
            ring.append(pltpu.VMEM((2, 256 >> (2 * p), 256), f32))
    for c in range(4):
        for p in range(3):
            ring.append(pltpu.VMEM(row_dims(CHUNK_AXES[c][p + 1 :]) + (16, 512), f32))
    slab = pltpu.VMEM((4, 2, 4, 7, 3, 8, 128), bf16)
    return pl.pallas_call(
        functools.partial(sublayer_kernel, inv_root),
        out_shape=(
            jax.ShapeDtypeStruct((256, 1024), bf16),
            jax.ShapeDtypeStruct((256, 1024), bf16),
            jax.ShapeDtypeStruct((8, 4096), f32),
        ),
        in_specs=[any_space] + [vmem] * 4,
        out_specs=(vmem,) * 3,
        scratch_shapes=[
            pltpu.VMEM((256, 1024), bf16),
            pltpu.VMEM((4, 64, 1024), bf16),
            pltpu.VMEM((256, 1), f32),
            pltpu.VMEM((4, 64, 1024), bf16),
            pltpu.VMEM((4, 64, 3072), bf16),
            pltpu.VMEM((1024, 4096), bf16),
            pltpu.VMEM((256, 1024), f32),
            pltpu.VMEM((4, 2, 28, 32, 256), bf16),
            pltpu.VMEM((4, 64, 1024), bf16),
            pltpu.VMEM((4, 64, 1024), bf16),
            pltpu.VMEM((4, 512, 256), f32),
            pltpu.VMEM((4, 2, 28, 32, 256), f32),
            slab, slab, slab, slab,
            pltpu.VMEM((4, 2, 2, 6, 16, 256), bf16),
            pltpu.VMEM((4, 2, 2, 6, 16, 256), bf16),
            pltpu.VMEM((2, 4, 2, 4, 2, 16, 256), bf16),
            pltpu.VMEM((2, 4, 2, 4, 2, 16, 256), bf16),
            pltpu.VMEM((4, 2, 4, 64, 256), bf16),
            pltpu.VMEM((4, 8, 512), f32),
            pltpu.VMEM((4, 8, 512), f32),
            dma((10,)),
        ]
        + [dma((4, 2))] * 4
        + [dma((4,))] * 8
        + [dma((3, 4))] * 2
        + [dma((4, 2))] * 2
        + [dma((4, 3, 6))] * 2
        + ring,
        compiler_params=pltpu.CompilerParams(
            collective_id=0, has_side_effects=True, vmem_limit_bytes=67043328
        ),
    )(weights, tokens, cotangent, tissue, gain)


def place_kernel(*refs):
    for source, target in zip(refs[:3], refs[3:]):
        target[...] = source[...]


def place(*arrays):
    vmem = pl.BlockSpec(memory_space=pltpu.VMEM)
    return pl.pallas_call(
        place_kernel,
        out_shape=tuple(jax.ShapeDtypeStruct(a.shape, a.dtype) for a in arrays),
        in_specs=[vmem] * 3,
        out_specs=(vmem,) * 3,
    )(*arrays)


def local(tokens, weights, norm_gain, tissue, cotangent):
    model_width = tokens.shape[-1]
    token_count = tokens.shape[1] * tokens.shape[2]
    group_count = lax.axis_size("slide") * lax.axis_size("gy") * lax.axis_size("gx")
    inv_root = 1.0 / math.sqrt(group_count * token_count)
    block_output, input_grad, weight_grads = sublayer(
        weights,
        tokens.reshape(token_count, model_width),
        cotangent.reshape(token_count, model_width),
        tissue[0],
        norm_gain.reshape(1, model_width),
        inv_root,
    )
    block_output, input_grad, weight_grads = place(block_output, input_grad, weight_grads)
    return (block_output.reshape(tokens.shape), input_grad.reshape(tokens.shape), weight_grads)


def solution(mesh):
    in_specs = (
        P("slide", "gy", "gx", None),
        P(),
        P(),
        P("slide", "gy", "gx"),
        P("slide", "gy", "gx", None),
    )
    out_specs = (
        P("slide", "gy", "gx", None),
        P("slide", "gy", "gx", None),
        P(("slide", "gy", "gx"), None),
    )
    return jax.shard_map(local, mesh=mesh, in_specs=in_specs, out_specs=out_specs, check_vma=False)
```
